32 devices in a mesh: blk: 8 (over z, x), mp: 4 (over y, core).
Axes of the slice: x: 2, y: 2, z: 4, core: 2. Of those that a mesh axis runs over, the one named last changes fastest.
Arguments:
- lengths: int32 [4], replicated, may hold values from 1 to 512, 1024 in all
- groups: int32 [4], replicated, may hold values from 0 to 3, as said below
- deal: int32 [1024], P('blk'), may hold values from 0 to 1023, as said below
- prefix_block: int32 [8], P('blk'), may hold values from 0 to 7, each once
- queries: bfloat16 [1024, 2048], P('blk', 'mp'), may hold values from -8 to 8
- keys: bfloat16 [1024, 512], P('blk', 'mp'), may hold values from -8 to 8
- values: bfloat16 [1024, 512], P('blk', 'mp'), may hold values from -6 to 6
- prefix_key_blocks: bfloat16 [512, 512], P('blk', 'mp'), may hold values from -8 to 8
- prefix_value_blocks: bfloat16 [512, 512], P('blk', 'mp'), may hold values from -6 to 6
- out_weight: bfloat16 [2048, 4096], P('mp'), may hold values from -0.125 to 0.125
Outputs:
- layer_out: bfloat16 [1024, 4096], P('blk', 'mp')
The draws below stay inside these ranges and needn't reach their ends.
Inputs may be any that keep to these rules, and one draw needn't show every extreme that they name: The 4 lengths sum to 1024; the largest is 512. `groups`: each group has exactly 1 request. `deal`: a permutation of the request-order rows; on every index of blk, the 16 slots c * 16 to c * 16 + 15 hold rows taken from request-order rows c * 128 to c * 128 + 127, and over all indices of blk each of those rows appears once. `prefix_block`: a permutation of the blocks.
All inputs are finite; a program needn't handle non-finite values.
Results may differ from the reference program's by a relative error of at most 0.012.
Values may be sent and summed in bfloat16 or wider, within the bound.
A program may use at most 64 MiB of HBM per device.

```python
import math
import jax
import jax.numpy as jnp
import numpy as np
from jax import lax

D = 4096
QUERY_HEADS = 16
KEY_VALUE_HEADS = 4
HEAD_WIDTH = 128
GROUPS = 4
TOK_DEV = 128
BLOCK_PREFIX_LEN = 64
PREFIX_BLOCKS = 8
SUFFIX_TOKENS = 1024
REQS = 4
LONGEST = 512


def draw_groups(key, part):
    shuffled = jax.random.permutation(jax.random.fold_in(key, 11), REQS)
    return (shuffled % GROUPS).astype(jnp.int32)


def draw_deal(key, part):
    piece_rows = TOK_DEV // PREFIX_BLOCKS
    base_key = jax.random.fold_in(key, 23)

    def shuffle_one(source_index):
        return jax.random.permutation(jax.random.fold_in(base_key, source_index), TOK_DEV)
    shuffles = jax.vmap(shuffle_one)(jnp.arange(PREFIX_BLOCKS))
    row_ids = shuffles.reshape(PREFIX_BLOCKS, PREFIX_BLOCKS, piece_rows) + (jnp.arange(PREFIX_BLOCKS) * TOK_DEV)[:, None, None]
    return jnp.transpose(row_ids, (1, 0, 2)).reshape(SUFFIX_TOKENS).astype(jnp.int32)


def draw_queries(key, part):
    array_shape = (SUFFIX_TOKENS, QUERY_HEADS * HEAD_WIDTH)
    sub_key = jax.random.fold_in(key, 37)
    drawn = jnp.clip(1.7 * jax.random.normal(sub_key, array_shape, jnp.float32), -8.0, 8.0)
    return drawn.astype(jnp.bfloat16)


def draw_prefix_key_blocks(key, part):
    array_shape = (PREFIX_BLOCKS * BLOCK_PREFIX_LEN, KEY_VALUE_HEADS * HEAD_WIDTH)
    sub_key = jax.random.fold_in(key, 41)
    drawn = jnp.clip(1.7 * jax.random.normal(sub_key, array_shape, jnp.float32), -8.0, 8.0)
    return drawn.astype(jnp.bfloat16)


def block_scale(key, shape, shards, low, top_value):
    loudness = 1.0
    for dim, shards_of in shards:
        draws = jax.random.uniform(jax.random.fold_in(jax.random.fold_in(key, 6), dim), (shards_of,), jnp.float32, low / len(shards), top_value / len(shards))
        loudness = loudness * jnp.repeat(jnp.exp(draws), shape[dim] // shards_of).reshape((-1,) + (1,) * (len(shape) - 1 - dim))
    return loudness


def profile(amount, total, limit, skew):
    loads = [(1 << 20) // math.isqrt(rank ** skew) + 1 for rank in range(2, amount + 1)]
    surplus, given = total - limit - (amount - 1), [1] * (amount - 1)
    while surplus > 0:
        movable = [i for i in range(amount - 1) if given[i] < limit]
        mass, left = sum([loads[i] for i in movable]), surplus
        for i in movable:
            more = min(limit - given[i], max(1, left * loads[i] // mass), surplus)
            given[i] = given[i] + more
            surplus = surplus - more
    return np.array([limit] + given)


def uneven(key, count, total, limit, slope):
    if count == 2:
        one = jax.random.randint(key, (), max(1, total - limit), min(limit, total - 1) + 1)
        return jnp.stack([one, total - one])
    sizes = jnp.asarray(profile(count, total, limit, slope), jnp.int32)
    pairs = (count - 1) // 2
    source_of, taker = sizes[1:1 + 2 * pairs:2], sizes[2:2 + 2 * pairs:2]
    slack = jnp.minimum(source_of - 1, limit - taker)
    passed = jax.random.randint(jax.random.fold_in(key, 1), (pairs,), 0, 1 << 20) % (slack + 1)
    sizes = sizes.at[1:1 + 2 * pairs:2].set(source_of - passed).at[2:2 + 2 * pairs:2].set(taker + passed)
    return sizes[jax.random.permutation(jax.random.fold_in(key, 2), count)]


def bell_draw(stream_key, dims, width, reach, cuts=(), kind=jnp.bfloat16):
    entries = width * jax.random.normal(stream_key, dims, jnp.float32)
    if cuts:
        entries = entries * block_scale(stream_key, dims, cuts, -0.22, 0.18)
    return jnp.clip(entries, -reach, reach).astype(kind)


def setup_inputs(seed: int = 0) -> dict:
    seeds = jax.random.split(jax.random.key(seed), 11)
    return {
        "lengths": uneven(seeds[0], REQS, SUFFIX_TOKENS, LONGEST, 2).astype(jnp.int32),
        "groups": draw_groups(jax.random.fold_in(seeds[10], 71), 0),
        "deal": draw_deal(jax.random.fold_in(seeds[10], 71), 0),
        "prefix_block": jax.random.permutation(seeds[3], PREFIX_BLOCKS).astype(jnp.int32),
        "queries": draw_queries(jax.random.fold_in(seeds[10], 71), 0),
        "keys": bell_draw(seeds[5], (SUFFIX_TOKENS, KEY_VALUE_HEADS * HEAD_WIDTH), 1.7, 8.0, ((0, 8), (1, 4))),
        "values": bell_draw(seeds[6], (SUFFIX_TOKENS, KEY_VALUE_HEADS * HEAD_WIDTH), 1.0, 6.0, ((0, 8), (1, 4))),
        "prefix_key_blocks": draw_prefix_key_blocks(jax.random.fold_in(seeds[10], 71), 0),
        "prefix_value_blocks": bell_draw(seeds[8], (PREFIX_BLOCKS * BLOCK_PREFIX_LEN, KEY_VALUE_HEADS * HEAD_WIDTH), 1.0, 6.0, ((0, 8), (1, 4))),
        "out_weight": bell_draw(seeds[9], (QUERY_HEADS * HEAD_WIDTH, D), (QUERY_HEADS * HEAD_WIDTH) ** -0.5, 0.125, ((0, 4),)),
    }


NEGATIVE = -1e+30

def request_of(row_ids, req_ends):
    return lax.optimization_barrier(jnp.sum((row_ids[:, None] >= req_ends[None, :]).astype(jnp.int32), axis=1)).astype(jnp.int32)

def reference(lengths, groups, deal, prefix_block, queries, keys, values, prefix_key_blocks, prefix_value_blocks, out_weight):
    sorted_queries = jnp.zeros_like(queries).at[deal].set(queries)
    sorted_keys = jnp.zeros_like(keys).at[deal].set(keys)
    sorted_values = jnp.zeros_like(values).at[deal].set(values)
    req_ends = jnp.cumsum(lengths).astype(jnp.int32)
    row_ids = jnp.arange(SUFFIX_TOKENS, dtype=jnp.int32)
    row_req = request_of(row_ids, req_ends)
    row_group = groups[row_req].astype(jnp.int32)
    key_group = (jnp.repeat(prefix_block, BLOCK_PREFIX_LEN) // (PREFIX_BLOCKS // GROUPS)).astype(jnp.int32)
    query_per_key_head = QUERY_HEADS // KEY_VALUE_HEADS
    stored_keys = prefix_key_blocks.astype(jnp.float32).reshape(-1, KEY_VALUE_HEADS, HEAD_WIDTH)
    stored_values = prefix_value_blocks.astype(jnp.float32).reshape(-1, KEY_VALUE_HEADS, HEAD_WIDTH)
    stretch_keys = min(LONGEST + 512, SUFFIX_TOKENS)
    score_scale = 1.0 / math.sqrt(HEAD_WIDTH)

    def one_block(block_index):
        row_begin = (block_index * 512).astype(jnp.int32)
        key_begin = jnp.clip(row_begin + 512 - stretch_keys, 0, SUFFIX_TOKENS - stretch_keys).astype(jnp.int32)
        query_float = lax.dynamic_slice_in_dim(sorted_queries, row_begin, 512, 0).astype(jnp.float32).reshape(512, KEY_VALUE_HEADS, query_per_key_head, HEAD_WIDTH)
        suffix_key_rows = lax.dynamic_slice_in_dim(sorted_keys, key_begin, stretch_keys, 0).astype(jnp.float32).reshape(stretch_keys, KEY_VALUE_HEADS, HEAD_WIDTH)
        suffix_value_rows = lax.dynamic_slice_in_dim(sorted_values, key_begin, stretch_keys, 0).astype(jnp.float32).reshape(stretch_keys, KEY_VALUE_HEADS, HEAD_WIDTH)
        query_rows = row_begin + jnp.arange(512, dtype=jnp.int32)
        key_rows = key_begin + jnp.arange(stretch_keys, dtype=jnp.int32)
        query_req = lax.dynamic_slice_in_dim(row_req, row_begin, 512, 0)
        query_group = lax.dynamic_slice_in_dim(row_group, row_begin, 512, 0)
        key_req = lax.dynamic_slice_in_dim(row_req, key_begin, stretch_keys, 0)
        own_mask = (key_req[None, :] == query_req[:, None]) & (key_rows[None, :] <= query_rows[:, None])
        cache_mask = key_group[None, :] == query_group[:, None]
        all_keys = jnp.concatenate([stored_keys, suffix_key_rows], axis=0)
        all_values = jnp.concatenate([stored_values, suffix_value_rows], axis=0)
        visible = jnp.concatenate([cache_mask, own_mask], axis=1)[:, None, None, :]
        scores = jnp.einsum('qgjd,ngd->qgjn', query_float, all_keys) * score_scale
        scores = jnp.where(visible, scores, NEGATIVE)
        row_top = lax.optimization_barrier(jnp.max(scores, axis=3, keepdims=True))
        weights = jnp.where(visible, jnp.exp(scores - row_top), 0.0)
        total = lax.optimization_barrier(jnp.sum(weights, axis=3))
        rounded = lax.optimization_barrier(weights.astype(jnp.bfloat16))
        mixed = jnp.einsum('qgjn,ngd->qgjd', rounded.astype(jnp.float32), all_values)
        return (mixed / total[..., None]).reshape(512, QUERY_HEADS * HEAD_WIDTH).astype(jnp.bfloat16)
    attended = lax.map(one_block, jnp.arange(SUFFIX_TOKENS // 512)).reshape(SUFFIX_TOKENS, QUERY_HEADS * HEAD_WIDTH)
    return jnp.dot(attended, out_weight, preferred_element_type=jnp.float32).astype(jnp.bfloat16)
```

```python
import functools
import math

import jax
import jax.numpy as jnp
from jax import lax
from jax.experimental import pallas as pl
from jax.experimental.pallas import tpu as pltpu
from jax.sharding import PartitionSpec as P

HEAD_WIDTH = 128
GROUPS = 4


NEGATIVE = -1e30


def request_index(row_ids, req_ends):
    return jnp.sum((row_ids[:, None] >= req_ends[None, :]).astype(jnp.int32), axis=1)


def lookup(values_table, indices):
    slots = jnp.arange(values_table.shape[0], dtype=jnp.int32)
    return jnp.sum(jnp.where(indices[:, None] == slots[None, :], values_table[None, :], 0), axis=1)


def attend(flash_state, grouped, key_block, value_block, visible):
    run_best, run_total, run_accum = flash_state
    key_count = key_block.shape[0]
    kv_heads = grouped.shape[1]
    head_size = grouped.shape[3]
    score_scale = 1.0 / math.sqrt(head_size)
    keys_three = key_block.reshape(key_count, kv_heads, head_size)
    values_three = value_block.reshape(key_count, kv_heads, head_size)
    scores = (
        jnp.einsum("rgjd,ngd->rgjn", grouped, keys_three, preferred_element_type=jnp.float32)
        * score_scale
    )
    shown = visible[:, None, None, :]
    scores = jnp.where(shown, scores, NEGATIVE)
    new_best = jnp.maximum(run_best, jnp.max(scores, axis=3))
    weights = jnp.where(shown, jnp.exp(scores - new_best[..., None]), 0.0)
    factor = jnp.exp(run_best - new_best)
    run_total = run_total * factor + jnp.sum(weights, axis=3)
    mixed = jnp.einsum(
        "rgjn,ngd->rgjd",
        weights.astype(jnp.bfloat16),
        values_three,
        preferred_element_type=jnp.float32,
    )
    run_accum = run_accum * factor[..., None] + mixed
    return (new_best, run_total, run_accum)


def sweep(flash_state, grouped, key_block, value_block, key_info, visible_of):
    key_count = key_block.shape[0]
    step_width = key_count if key_count <= 1024 else math.gcd(key_count, 512)
    if step_width == key_count:
        return attend(flash_state, grouped, key_block, value_block, visible_of(key_info))

    def one_step(carried, step_index):
        offset = step_index * step_width
        key_part = lax.dynamic_slice_in_dim(key_block, offset, step_width, 0)
        value_part = lax.dynamic_slice_in_dim(value_block, offset, step_width, 0)
        info_part = lax.dynamic_slice_in_dim(key_info, offset, step_width, 0)
        return (attend(carried, grouped, key_part, value_part, visible_of(info_part)), None)

    flash_state, _ = lax.scan(
        one_step, flash_state, jnp.arange(key_count // step_width, dtype=jnp.int32)
    )
    return flash_state


def plain_shards(
    lengths,
    groups,
    deal,
    prefix_block,
    queries,
    keys,
    values,
    prefix_key_blocks,
    prefix_value_blocks,
    out_weight,
):
    count_rows = queries.shape[0]
    kv_heads = keys.shape[1] // HEAD_WIDTH
    query_per_key_head = queries.shape[1] // keys.shape[1]
    devices = lax.axis_size("blk")
    my_index = lax.axis_index("blk")
    piece_rows = count_rows // devices
    per_group = devices // GROUPS
    prefix_rows = prefix_key_blocks.shape[0]
    ranks = jnp.arange(lengths.shape[0], dtype=jnp.int32)
    req_ends = jnp.sum(
        jnp.where(ranks[:, None] >= ranks[None, :], lengths[None, :], 0), axis=1
    ).astype(jnp.int32)
    arrived = lax.all_to_all(
        deal.reshape(devices, piece_rows), "blk", split_axis=0, concat_axis=0, tiled=True
    )
    placed = arrived.reshape(count_rows) - my_index * count_rows

    def prefix_pass(flash_state, grouped, query_group, block_ids):

        def prefix_step(carried, kv_piece):
            key_count = kv_piece[0].shape[0]
            key_group = jnp.broadcast_to(
                (block_ids // per_group)[:, None], (key_count // prefix_rows, prefix_rows)
            ).reshape(key_count)

            def same_group(key_info):
                return key_info[None, :] == query_group[:, None]

            return sweep(carried, grouped, kv_piece[0], kv_piece[1], key_group, same_group)

        return prefix_step(
            flash_state,
            (
                lax.all_gather(prefix_key_blocks, "blk", axis=0, tiled=True),
                lax.all_gather(prefix_value_blocks, "blk", axis=0, tiled=True),
            ),
        )

    def suffix_rule(query_rows, query_req):

        def same_request(key_info):
            key_req = request_index(key_info, req_ends)
            return (
                (key_info[None, :] >= 0)
                & (key_req[None, :] == query_req[:, None])
                & (key_info[None, :] <= query_rows[:, None])
            )

        return same_request

    key_rows, block_ids = (
        lax.all_gather(deal, "blk", axis=0, tiled=True),
        lax.all_gather(prefix_block, "blk", axis=0, tiled=True),
    )
    query_rows = deal
    query_req = request_index(query_rows, req_ends)
    query_group = lookup(groups, query_req)
    grouped = queries.reshape(count_rows, kv_heads, query_per_key_head, HEAD_WIDTH)
    flash_state = prefix_pass(
        (
            jnp.full((count_rows, kv_heads, query_per_key_head), NEGATIVE, jnp.float32),
            jnp.zeros((count_rows, kv_heads, query_per_key_head), jnp.float32),
            jnp.zeros((count_rows, kv_heads, query_per_key_head, HEAD_WIDTH), jnp.float32),
        ),
        grouped,
        query_group,
        block_ids,
    )
    visible_of = suffix_rule(query_rows, query_req)
    kv_piece = (
        lax.all_gather(keys, "blk", axis=0, tiled=True),
        lax.all_gather(values, "blk", axis=0, tiled=True),
    )
    key_info = key_rows
    flash_state = sweep(flash_state, grouped, kv_piece[0], kv_piece[1], key_info, visible_of)
    run_best, run_total, run_accum = flash_state
    attended = (run_accum / run_total[..., None]).astype(jnp.bfloat16).reshape(count_rows, -1)
    returned = lax.all_to_all(
        attended.reshape(devices, piece_rows, -1), "blk", split_axis=0, concat_axis=0, tiled=True
    )
    flat = returned.reshape(count_rows, returned.shape[2])
    turn = placed[None, :] == jnp.arange(count_rows, dtype=jnp.int32)[:, None]
    ordered = jnp.dot(
        turn.astype(flat.dtype), flat, preferred_element_type=jnp.float32
    ).astype(flat.dtype)
    partial_value = jnp.dot(ordered, out_weight, preferred_element_type=jnp.float32)
    return lax.psum_scatter(
        partial_value.astype(jnp.bfloat16), "mp", scatter_dimension=1, tiled=True
    )


LOG2E = 1.4426950408889634


def fused_kernel(
    n,
    lengths_hbm,
    groups_hbm,
    block_hbm,
    deal_hbm,
    q_hbm,
    k_hbm,
    v_hbm,
    pk_hbm,
    pv_hbm,
    w_hbm,
    out_ref,
    lengths_ref,
    groups_ref,
    block_ref,
    q_buf,
    ordered_q,
    k_buf,
    v_buf,
    w_own,
    w_sib,
    meta_buf,
    score_buf,
    weight_buf,
    att_buf,
    att_sib,
    part_buf,
    send_buf,
    recv_buf,
    local_sem,
    w_sem,
    ready_blk,
    ready_mp,
    z_send,
    x_send,
    f_send,
    kv_recv,
    meta_send,
    meta_recv,
    q_send,
    q_recv,
    wx_send,
    wx_recv,
    att_send,
    att_recv,
    red_send,
    red_recv,
):
    me = lax.axis_index("blk")
    m = lax.axis_index("mp")
    y = m // 2
    c = m - y * 2
    sibling = y * 2 + (1 - c)
    across = (1 - y) * 2 + c
    diagonal = (1 - y) * 2 + (1 - c)
    z = me // 2
    x = me - z * 2
    partner = z * 2 + 1 - x
    rows = q_hbm.shape[0]
    heads = q_hbm.shape[1] // HEAD_WIDTH
    piece = rows // n
    requests = lengths_hbm.shape[0]
    per_group = n // GROUPS
    width = out_ref.shape[1]
    lines = n // 2
    MESH = pl.DeviceIdType.MESH
    prefix_rows = pk_hbm.shape[0]
    lead = 3 * piece
    rest = lead + prefix_rows
    held = rows + prefix_rows

    def plane_window(t):
        if t < lines // 2:
            return pl.ds(0, held - 4 * piece)
        return pl.ds((t - lines // 2) * 2 * piece, held - 2 * piece)

    def block_window(block, low):
        if low:
            return pl.ds(0, held - 4 * piece)
        first = jnp.maximum(block - n // 2, 0) * piece
        return pl.ds(pl.multiple_of(first, piece), held - lead)

    bufs = (k_buf, v_buf)
    local = [
        pltpu.make_async_copy(k_hbm.at[0:lead], k_buf.at[me, 0:lead], local_sem.at[0]),
        pltpu.make_async_copy(pk_hbm, k_buf.at[me, lead:rest], local_sem.at[1]),
        pltpu.make_async_copy(k_hbm.at[lead:], k_buf.at[me, rest:], local_sem.at[2]),
        pltpu.make_async_copy(v_hbm.at[0:lead], v_buf.at[me, 0:lead], local_sem.at[3]),
        pltpu.make_async_copy(pv_hbm, v_buf.at[me, lead:rest], local_sem.at[4]),
        pltpu.make_async_copy(v_hbm.at[lead:], v_buf.at[me, rest:], local_sem.at[5]),
        pltpu.make_async_copy(deal_hbm, meta_buf.at[me, 0:1], local_sem.at[6]),
        pltpu.make_async_copy(block_hbm, block_ref, local_sem.at[7]),
    ]
    late = [
        pltpu.make_async_copy(lengths_hbm, lengths_ref, local_sem.at[8]),
        pltpu.make_async_copy(groups_hbm, groups_ref, local_sem.at[9]),
        pltpu.make_async_copy(
            q_hbm.at[pl.ds(pl.multiple_of(me * piece, piece), piece)],
            q_buf.at[me],
            local_sem.at[10],
        ),
    ]
    for s in range(n):

        @pl.when(me != s)
        def _(s=s):
            k_buf[s] = jnp.zeros((held, HEAD_WIDTH), jnp.bfloat16)
            v_buf[s] = jnp.zeros((held, HEAD_WIDTH), jnp.bfloat16)

    barrier = pltpu.get_barrier_semaphore()
    for t in range(n):

        @pl.when(me < t)
        def _(t=t):
            pl.semaphore_signal(barrier, inc=1, device_id={"blk": t}, device_id_type=MESH)

    @pl.when(y == 0)
    def _():
        pl.semaphore_signal(barrier, inc=1, device_id={"mp": across}, device_id_type=MESH)

    @pl.when(c == 1)
    def _():
        pl.semaphore_signal(barrier, inc=1, device_id={"mp": sibling}, device_id_type=MESH)

    for copy in local + late:
        copy.start()
    before = me + y + (1 - c)

    @pl.when(before > 0)
    def _():
        pl.semaphore_wait(barrier, before)

    for t in range(n):

        @pl.when(t < me)
        def _(t=t):
            pl.semaphore_signal(
                ready_blk.at[me], inc=1, device_id={"blk": t}, device_id_type=MESH
            )

    @pl.when(c == 0)
    def _():
        pl.semaphore_signal(
            ready_mp.at[0], inc=1, device_id={"mp": sibling}, device_id_type=MESH
        )

    @pl.when(y == 1)
    def _():
        pl.semaphore_signal(
            ready_mp.at[1], inc=1, device_id={"mp": across}, device_id_type=MESH
        )

    for copy in local:
        copy.wait()
    meta_buf[me, 1:2, :] = jnp.full((1, rows), block_ref[0] // per_group, jnp.int32)

    def kv_copy(part, slot, window, target, sem):
        return pltpu.make_async_remote_copy(
            src_ref=bufs[part].at[slot, window],
            dst_ref=bufs[part].at[slot, window],
            send_sem=sem,
            recv_sem=kv_recv.at[slot, part],
            device_id={"blk": target},
            device_id_type=MESH,
        )

    def plane_copy(part, t):
        whole = t == 2
        window = pl.ds(0, held) if whole else plane_window(t)
        return kv_copy(part, me, window, 2 * t + x, z_send.at[t, part])

    def cross_copy(part, zz, low):
        slot = 2 * zz + x
        return kv_copy(part, slot, block_window(partner, low), partner, x_send.at[zz, part])

    def pass_copy(part, zz):
        return kv_copy(part, 2 * zz + x, plane_window(3), 6 + x, f_send.at[zz, part])

    def cross(part, zz, act):
        @pl.when(z < lines // 2)
        def _():
            act(cross_copy(part, zz, True))

        @pl.when(z >= lines // 2)
        def _():
            act(cross_copy(part, zz, False))

    def meta_copy(t):
        return pltpu.make_async_remote_copy(
            src_ref=meta_buf.at[me],
            dst_ref=meta_buf.at[me],
            send_sem=meta_send.at[t],
            recv_sem=meta_recv.at[me],
            device_id={"blk": t},
            device_id_type=MESH,
        )

    def q_copy(t):
        return pltpu.make_async_remote_copy(
            src_ref=q_hbm.at[t * piece : (t + 1) * piece],
            dst_ref=q_buf.at[me],
            send_sem=q_send.at[t],
            recv_sem=q_recv.at[me],
            device_id={"blk": t},
            device_id_type=MESH,
        )

    def start(copy):
        copy.start()

    def sent(copy):
        copy.wait_send()

    def to_plane(t, act):
        @pl.when((z != t) & ((t != 3) | (z == 2)))
        def _():
            for part in range(2):
                act(plane_copy(part, t))

    for t in range(lines - 1):

        @pl.when(t < z)
        def _(t=t):
            to_plane(t, start)
            for xx in range(2):
                meta_copy(2 * t + xx).start()
            for xx in range(2):
                q_copy(2 * t + xx).start()

    @pl.when(x == 0)
    def _():
        pl.semaphore_wait(ready_blk.at[me + 1], 1)

    for part in range(2):
        cross(part, z, start)
    for t in range(n):

        @pl.when(partner == t)
        def _(t=t):
            meta_copy(t).start()
            q_copy(t).start()

    for t in range(1, lines):

        @pl.when(z < t)
        def _(t=t):
            for xx in range(2):
                pl.semaphore_wait(ready_blk.at[2 * t + xx], 1)
            to_plane(t, start)
            for xx in range(2):
                meta_copy(2 * t + xx).start()
            for xx in range(2):
                q_copy(2 * t + xx).start()

    @pl.when(c == 1)
    def _():
        pl.semaphore_wait(ready_mp.at[0], 1)

    def columns(block):
        return pl.ds(pl.multiple_of(block * width, 128), width)

    w_out = [
        pltpu.make_async_remote_copy(
            src_ref=w_hbm.at[:, columns(block)],
            dst_ref=w_sib.at[i],
            send_sem=wx_send.at[i],
            recv_sem=wx_recv.at[i],
            device_id={"mp": sibling},
            device_id_type=MESH,
        )
        for i, block in enumerate((diagonal, sibling))
    ]
    w_in = [
        pltpu.make_async_copy(w_hbm.at[:, columns(block)], w_own.at[i], w_sem.at[i])
        for i, block in enumerate((across, m))
    ]
    for copy in w_out + w_in:
        copy.start()

    def landed(part, zz, xx, own):
        slot = 2 * zz + xx
        if own:

            @pl.when(z == 2)
            def _():
                kv_copy(part, slot, pl.ds(0, held), partner, z_send.at[0, part]).wait_recv()

            @pl.when(z == 3)
            def _():
                kv_copy(part, slot, plane_window(3), partner, z_send.at[0, part]).wait_recv()

            @pl.when(z < 2)
            def _():
                kv_copy(part, slot, plane_window(0), partner, z_send.at[0, part]).wait_recv()

        else:

            @pl.when(z < 2)
            def _():
                kv_copy(
                    part, slot, block_window(me, True), partner, z_send.at[0, part]
                ).wait_recv()

            @pl.when(z >= 2)
            def _():
                kv_copy(
                    part, slot, block_window(me, False), partner, z_send.at[0, part]
                ).wait_recv()

    def relay(zz):
        for part in range(2):
            landed(part, zz, x, True)

            @pl.when((z == 2) & (zz < 2))
            def _(part=part):
                pass_copy(part, zz).start()

            cross(part, zz, start)

    for distance in range(1, lines):

        @pl.when(z >= distance)
        def _(distance=distance):
            relay(z - distance)

        @pl.when(z + distance < lines)
        def _(distance=distance):
            relay(z + distance)

    for copy in late:
        copy.wait()
    row_ids = lax.broadcasted_iota(jnp.int32, (rows, rows), 0) + me * rows
    start_row = jnp.zeros((rows, rows), jnp.int32)
    group_row = jnp.full((rows, rows), groups_ref[0], jnp.int32)
    end = lengths_ref[0]
    for r in range(1, requests):
        past = row_ids >= end
        start_row = jnp.where(past, end, start_row)
        group_row = jnp.where(past, groups_ref[r], group_row)
        end = end + lengths_ref[r]

    lane = lax.broadcasted_iota(jnp.int32, (1, rows), 1)
    query_row = jnp.zeros((1, rows), jnp.int32)
    for s in range(n):

        @pl.when(me != s)
        def _(s=s):
            pltpu.make_async_remote_copy(
                src_ref=meta_buf.at[s],
                dst_ref=meta_buf.at[s],
                send_sem=meta_send.at[s],
                recv_sem=meta_recv.at[s],
                device_id={"blk": partner},
                device_id_type=MESH,
            ).wait_recv()

        shift = lax.rem((s + n - me) * piece, rows)
        turned = pltpu.roll(meta_buf[s], shift, 1)[0:1, :]
        query_row = jnp.where((lane >= s * piece) & (lane < (s + 1) * piece), turned, query_row)
    select = jnp.where(row_ids == query_row, 1.0, 0.0).astype(jnp.bfloat16)
    for s in range(n):

        @pl.when(me != s)
        def _(s=s):
            pltpu.make_async_remote_copy(
                src_ref=q_buf.at[s],
                dst_ref=q_buf.at[s],
                send_sem=q_send.at[s],
                recv_sem=q_recv.at[s],
                device_id={"blk": partner},
                device_id_type=MESH,
            ).wait_recv()

    placed = jnp.dot(
        select, q_buf[...].reshape(rows, -1), preferred_element_type=jnp.float32
    ).astype(jnp.bfloat16)
    for h in range(heads):
        ordered_q[h * rows : (h + 1) * rows, :] = placed[:, h * HEAD_WIDTH : (h + 1) * HEAD_WIDTH]
    scale = LOG2E / math.sqrt(HEAD_WIDTH)

    for zz in range(lines):
        landed(0, zz, 1 - x, False)
    blocks = n + n // 2
    top = None
    for b in range(blocks):
        if b < n:
            keys = jnp.concatenate([k_buf[b, 0:lead], k_buf[b, rest:]], axis=0)
            key_row = meta_buf[b, 0:1, :]
            shown = (key_row >= start_row) & (key_row <= row_ids)
        else:
            r = b - n
            keys = k_buf[2 * r : 2 * r + 2, lead:rest].reshape(rows, HEAD_WIDTH)
            key_group = jnp.where(
                lane < rows // 2, meta_buf[2 * r, 1:2, :], meta_buf[2 * r + 1, 1:2, :]
            )
            shown = key_group == group_row
        scores = (
            lax.dot_general(
                ordered_q[...],
                keys,
                (((1,), (1,)), ((), ())),
                preferred_element_type=jnp.float32,
            )
            * scale
        )
        scores = jnp.where(shown[None], scores.reshape(heads, rows, rows), NEGATIVE)
        score_buf[b] = scores
        top = scores if top is None else jnp.maximum(top, scores)
    top = jnp.max(top, axis=2, keepdims=True)

    for zz in range(lines):
        landed(1, zz, 1 - x, False)
    total = jnp.zeros((heads, rows, rows), jnp.float32)
    for b in range(blocks):
        weights = jnp.exp2(score_buf[b] - top)
        total = total + weights
        weight_buf[:, b * rows : (b + 1) * rows] = weights.astype(jnp.bfloat16).reshape(
            heads * rows, rows
        )
    total = jnp.sum(total, axis=2, keepdims=True).reshape(heads * rows, 1)
    suffix = jnp.concatenate([v_buf[:, 0:lead], v_buf[:, rest:]], axis=1)
    mixed = jnp.dot(
        weight_buf[:, : n * rows],
        suffix.reshape(n * rows, HEAD_WIDTH),
        preferred_element_type=jnp.float32,
    ) + jnp.dot(
        weight_buf[:, n * rows :],
        v_buf[:, lead:rest].reshape(n * rows // 2, HEAD_WIDTH),
        preferred_element_type=jnp.float32,
    )
    mixed = (mixed / total).astype(jnp.bfloat16)
    for h in range(heads):
        att_buf[:, h * HEAD_WIDTH : (h + 1) * HEAD_WIDTH] = mixed[h * rows : (h + 1) * rows]

    att_copy = pltpu.make_async_remote_copy(
        src_ref=att_buf,
        dst_ref=att_sib,
        send_sem=att_send,
        recv_sem=att_recv,
        device_id={"mp": sibling},
        device_id_type=MESH,
    )
    att_copy.start()

    @pl.when(y == 0)
    def _():
        pl.semaphore_wait(ready_mp.at[1], 1)

    chunks = send_buf.shape[0]
    span = width // chunks
    for i in range(2):
        w_in[i].wait()
        w_out[i].wait_recv()
    att_copy.wait_recv()

    def project(i, lanes):
        return jnp.dot(
            att_buf[...], w_own[i, :, lanes], preferred_element_type=jnp.float32
        ) + jnp.dot(att_sib[...], w_sib[i, :, lanes], preferred_element_type=jnp.float32)

    red_copies = []
    for j in range(chunks):
        lanes = slice(j * span, (j + 1) * span)
        send_buf[j] = project(0, lanes).astype(jnp.bfloat16)
        copy = pltpu.make_async_remote_copy(
            src_ref=send_buf.at[j],
            dst_ref=recv_buf.at[j],
            send_sem=red_send.at[j],
            recv_sem=red_recv.at[j],
            device_id={"mp": across},
            device_id_type=MESH,
        )
        copy.start()
        red_copies.append(copy)
    for j in range(chunks):
        part_buf[j] = project(1, slice(j * span, (j + 1) * span))
    for j in range(chunks):
        red_copies[j].wait_recv()
        out_ref[:, j * span : (j + 1) * span] = (
            part_buf[j] + recv_buf[j].astype(jnp.float32)
        ).astype(jnp.bfloat16)

    for t in range(lines):
        to_plane(t, sent)
    for zz in range(lines):
        for part in range(2):
            cross(part, zz, sent)

            @pl.when((z == 2) & (zz < 2))
            def _(part=part, zz=zz):
                pass_copy(part, zz).wait_send()

    for t in range(n):

        @pl.when(me != t)
        def _(t=t):
            meta_copy(t).wait_send()
            q_copy(t).wait_send()

    for copy in w_out + red_copies + [att_copy]:
        copy.wait_send()


def shards(
    lengths,
    groups,
    deal,
    prefix_block,
    queries,
    keys,
    values,
    prefix_key_blocks,
    prefix_value_blocks,
    out_weight,
):
    n = lax.axis_size("blk")
    rows = queries.shape[0]
    piece = rows // n
    if n != 8 or rows != 128 or 2 * prefix_key_blocks.shape[0] != rows:
        return plain_shards(
            lengths,
            groups,
            deal,
            prefix_block,
            queries,
            keys,
            values,
            prefix_key_blocks,
            prefix_value_blocks,
            out_weight,
        )
    heads = queries.shape[1] // HEAD_WIDTH
    prefix_rows = prefix_key_blocks.shape[0]
    depth = out_weight.shape[0]
    columns = out_weight.shape[1] // lax.axis_size("mp")
    blocks = n + n // 2
    chunks = 4
    bf16, f32, i32 = jnp.bfloat16, jnp.float32, jnp.int32
    hbm = pl.BlockSpec(memory_space=pltpu.HBM)
    dma = pltpu.SemaphoreType.DMA
    regular = pltpu.SemaphoreType.REGULAR
    operands = (
        lengths,
        groups,
        jnp.broadcast_to(prefix_block, (rows,)),
        deal.reshape(1, rows),
        queries,
        keys,
        values,
        prefix_key_blocks,
        prefix_value_blocks,
        out_weight,
    )
    return pl.pallas_call(
        functools.partial(fused_kernel, n),
        out_shape=jax.ShapeDtypeStruct((rows, columns), bf16),
        in_specs=[hbm] * len(operands),
        out_specs=pl.BlockSpec(memory_space=pltpu.VMEM),
        scratch_shapes=[
            pltpu.SMEM(lengths.shape, i32),
            pltpu.SMEM(groups.shape, i32),
            pltpu.SMEM((rows,), i32),
            pltpu.VMEM((n, piece, queries.shape[1]), bf16),
            pltpu.VMEM((heads * rows, HEAD_WIDTH), bf16),
            pltpu.VMEM((n, rows + prefix_rows, HEAD_WIDTH), bf16),
            pltpu.VMEM((n, rows + prefix_rows, HEAD_WIDTH), bf16),
            pltpu.VMEM((2, depth, columns), bf16),
            pltpu.VMEM((2, depth, columns), bf16),
            pltpu.VMEM((n, 8, rows), i32),
            pltpu.VMEM((blocks, heads, rows, rows), f32),
            pltpu.VMEM((heads * rows, blocks * rows), bf16),
            pltpu.VMEM((rows, heads * HEAD_WIDTH), bf16),
            pltpu.VMEM((rows, heads * HEAD_WIDTH), bf16),
            pltpu.VMEM((chunks, rows, columns // chunks), f32),
            pltpu.VMEM((chunks, rows, columns // chunks), bf16),
            pltpu.VMEM((chunks, rows, columns // chunks), bf16),
            dma((11,)),
            dma((2,)),
            regular((n,)),
            regular((2,)),
            dma((n // 2, 2)),
            dma((n // 2, 2)),
            dma((n // 2, 2)),
            dma((n, 2)),
            dma((n,)),
            dma((n,)),
            dma((n,)),
            dma((n,)),
            dma((2,)),
            dma((2,)),
            dma,
            dma,
            dma((chunks,)),
            dma((chunks,)),
        ],
        compiler_params=pltpu.CompilerParams(
            collective_id=0, has_side_effects=True, vmem_limit_bytes=28 << 20
        ),
    )(*[pltpu.with_memory_space_constraint(v, pltpu.HBM) for v in operands])


def solution(mesh):
    return jax.shard_map(
        shards,
        mesh=mesh,
        in_specs=(
            P(),
            P(),
            P("blk"),
            P("blk"),
            P("blk", "mp"),
            P("blk", "mp"),
            P("blk", "mp"),
            P("blk", "mp"),
            P("blk", "mp"),
            P("mp", None),
        ),
        out_specs=P("blk", "mp"),
        check_vma=False,
    )
```

```python
import functools
import math

import jax
import jax.numpy as jnp
from jax import lax
from jax.experimental import pallas as pl
from jax.experimental.pallas import tpu as pltpu
from jax.sharding import PartitionSpec as P

HEAD_WIDTH = 128
GROUPS = 4


NEGATIVE = -1e30


def request_index(row_ids, req_ends):
    return jnp.sum((row_ids[:, None] >= req_ends[None, :]).astype(jnp.int32), axis=1)


def lookup(values_table, indices):
    slots = jnp.arange(values_table.shape[0], dtype=jnp.int32)
    return jnp.sum(jnp.where(indices[:, None] == slots[None, :], values_table[None, :], 0), axis=1)


def attend(flash_state, grouped, key_block, value_block, visible):
    run_best, run_total, run_accum = flash_state
    key_count = key_block.shape[0]
    kv_heads = grouped.shape[1]
    head_size = grouped.shape[3]
    score_scale = 1.0 / math.sqrt(head_size)
    keys_three = key_block.reshape(key_count, kv_heads, head_size)
    values_three = value_block.reshape(key_count, kv_heads, head_size)
    scores = (
        jnp.einsum("rgjd,ngd->rgjn", grouped, keys_three, preferred_element_type=jnp.float32)
        * score_scale
    )
    shown = visible[:, None, None, :]
    scores = jnp.where(shown, scores, NEGATIVE)
    new_best = jnp.maximum(run_best, jnp.max(scores, axis=3))
    weights = jnp.where(shown, jnp.exp(scores - new_best[..., None]), 0.0)
    factor = jnp.exp(run_best - new_best)
    run_total = run_total * factor + jnp.sum(weights, axis=3)
    mixed = jnp.einsum(
        "rgjn,ngd->rgjd",
        weights.astype(jnp.bfloat16),
        values_three,
        preferred_element_type=jnp.float32,
    )
    run_accum = run_accum * factor[..., None] + mixed
    return (new_best, run_total, run_accum)


def sweep(flash_state, grouped, key_block, value_block, key_info, visible_of):
    key_count = key_block.shape[0]
    step_width = key_count if key_count <= 1024 else math.gcd(key_count, 512)
    if step_width == key_count:
        return attend(flash_state, grouped, key_block, value_block, visible_of(key_info))

    def one_step(carried, step_index):
        offset = step_index * step_width
        key_part = lax.dynamic_slice_in_dim(key_block, offset, step_width, 0)
        value_part = lax.dynamic_slice_in_dim(value_block, offset, step_width, 0)
        info_part = lax.dynamic_slice_in_dim(key_info, offset, step_width, 0)
        return (attend(carried, grouped, key_part, value_part, visible_of(info_part)), None)

    flash_state, _ = lax.scan(
        one_step, flash_state, jnp.arange(key_count // step_width, dtype=jnp.int32)
    )
    return flash_state


def plain_shards(
    lengths,
    groups,
    deal,
    prefix_block,
    queries,
    keys,
    values,
    prefix_key_blocks,
    prefix_value_blocks,
    out_weight,
):
    count_rows = queries.shape[0]
    kv_heads = keys.shape[1] // HEAD_WIDTH
    query_per_key_head = queries.shape[1] // keys.shape[1]
    devices = lax.axis_size("blk")
    my_index = lax.axis_index("blk")
    piece_rows = count_rows // devices
    per_group = devices // GROUPS
    prefix_rows = prefix_key_blocks.shape[0]
    ranks = jnp.arange(lengths.shape[0], dtype=jnp.int32)
    req_ends = jnp.sum(
        jnp.where(ranks[:, None] >= ranks[None, :], lengths[None, :], 0), axis=1
    ).astype(jnp.int32)
    arrived = lax.all_to_all(
        deal.reshape(devices, piece_rows), "blk", split_axis=0, concat_axis=0, tiled=True
    )
    placed = arrived.reshape(count_rows) - my_index * count_rows

    def prefix_pass(flash_state, grouped, query_group, block_ids):

        def prefix_step(carried, kv_piece):
            key_count = kv_piece[0].shape[0]
            key_group = jnp.broadcast_to(
                (block_ids // per_group)[:, None], (key_count // prefix_rows, prefix_rows)
            ).reshape(key_count)

            def same_group(key_info):
                return key_info[None, :] == query_group[:, None]

            return sweep(carried, grouped, kv_piece[0], kv_piece[1], key_group, same_group)

        return prefix_step(
            flash_state,
            (
                lax.all_gather(prefix_key_blocks, "blk", axis=0, tiled=True),
                lax.all_gather(prefix_value_blocks, "blk", axis=0, tiled=True),
            ),
        )

    def suffix_rule(query_rows, query_req):

        def same_request(key_info):
            key_req = request_index(key_info, req_ends)
            return (
                (key_info[None, :] >= 0)
                & (key_req[None, :] == query_req[:, None])
                & (key_info[None, :] <= query_rows[:, None])
            )

        return same_request

    key_rows, block_ids = (
        lax.all_gather(deal, "blk", axis=0, tiled=True),
        lax.all_gather(prefix_block, "blk", axis=0, tiled=True),
    )
    query_rows = deal
    query_req = request_index(query_rows, req_ends)
    query_group = lookup(groups, query_req)
    grouped = queries.reshape(count_rows, kv_heads, query_per_key_head, HEAD_WIDTH)
    flash_state = prefix_pass(
        (
            jnp.full((count_rows, kv_heads, query_per_key_head), NEGATIVE, jnp.float32),
            jnp.zeros((count_rows, kv_heads, query_per_key_head), jnp.float32),
            jnp.zeros((count_rows, kv_heads, query_per_key_head, HEAD_WIDTH), jnp.float32),
        ),
        grouped,
        query_group,
        block_ids,
    )
    visible_of = suffix_rule(query_rows, query_req)
    kv_piece = (
        lax.all_gather(keys, "blk", axis=0, tiled=True),
        lax.all_gather(values, "blk", axis=0, tiled=True),
    )
    key_info = key_rows
    flash_state = sweep(flash_state, grouped, kv_piece[0], kv_piece[1], key_info, visible_of)
    run_best, run_total, run_accum = flash_state
    attended = (run_accum / run_total[..., None]).astype(jnp.bfloat16).reshape(count_rows, -1)
    returned = lax.all_to_all(
        attended.reshape(devices, piece_rows, -1), "blk", split_axis=0, concat_axis=0, tiled=True
    )
    flat = returned.reshape(count_rows, returned.shape[2])
    turn = placed[None, :] == jnp.arange(count_rows, dtype=jnp.int32)[:, None]
    ordered = jnp.dot(
        turn.astype(flat.dtype), flat, preferred_element_type=jnp.float32
    ).astype(flat.dtype)
    partial_value = jnp.dot(ordered, out_weight, preferred_element_type=jnp.float32)
    return lax.psum_scatter(
        partial_value.astype(jnp.bfloat16), "mp", scatter_dimension=1, tiled=True
    )


LOG2E = 1.4426950408889634


def fused_kernel(
    n,
    lengths_hbm,
    groups_hbm,
    block_ref,
    deal_hbm,
    q_hbm,
    k_hbm,
    v_hbm,
    pk_hbm,
    pv_hbm,
    w_hbm,
    out_ref,
    lengths_ref,
    groups_ref,
    q_buf,
    ordered_q,
    k_buf,
    v_buf,
    w_own,
    w_sib,
    meta_buf,
    score_buf,
    weight_buf,
    att_buf,
    att_sib,
    part_buf,
    send_buf,
    recv_buf,
    local_sem,
    w_sem,
    ready_blk,
    ready_mp,
    z_send,
    x_send,
    f_send,
    kv_recv,
    meta_send,
    meta_recv,
    q_send,
    q_recv,
    wx_send,
    wx_recv,
    att_send,
    att_recv,
    red_send,
    red_recv,
):
    me = lax.axis_index("blk")
    m = lax.axis_index("mp")
    y = m // 2
    c = m - y * 2
    sibling = y * 2 + (1 - c)
    across = (1 - y) * 2 + c
    diagonal = (1 - y) * 2 + (1 - c)
    z = me // 2
    x = me - z * 2
    partner = z * 2 + 1 - x
    rows = q_hbm.shape[0]
    heads = q_hbm.shape[1] // HEAD_WIDTH
    piece = rows // n
    requests = lengths_hbm.shape[0]
    per_group = n // GROUPS
    width = out_ref.shape[1]
    lines = n // 2
    MESH = pl.DeviceIdType.MESH
    prefix_rows = pk_hbm.shape[0]
    lead = 3 * piece
    rest = lead + prefix_rows
    held = rows + prefix_rows

    def plane_window(t):
        if t < lines // 2:
            return pl.ds(0, held - 4 * piece)
        return pl.ds((t - lines // 2) * 2 * piece, held - 2 * piece)

    def block_window(block, low):
        if low:
            return pl.ds(0, held - 4 * piece)
        first = jnp.maximum(block - n // 2, 0) * piece
        return pl.ds(pl.multiple_of(first, piece), held - lead)

    bufs = (k_buf, v_buf)
    local = [
        pltpu.make_async_copy(k_hbm.at[0:lead], k_buf.at[me, 0:lead], local_sem.at[0]),
        pltpu.make_async_copy(pk_hbm, k_buf.at[me, lead:rest], local_sem.at[1]),
        pltpu.make_async_copy(k_hbm.at[lead:], k_buf.at[me, rest:], local_sem.at[2]),
        pltpu.make_async_copy(v_hbm.at[0:lead], v_buf.at[me, 0:lead], local_sem.at[3]),
        pltpu.make_async_copy(pv_hbm, v_buf.at[me, lead:rest], local_sem.at[4]),
        pltpu.make_async_copy(v_hbm.at[lead:], v_buf.at[me, rest:], local_sem.at[5]),
        pltpu.make_async_copy(deal_hbm, meta_buf.at[me], local_sem.at[6]),
    ]
    late = [
        pltpu.make_async_copy(lengths_hbm, lengths_ref, local_sem.at[8]),
        pltpu.make_async_copy(groups_hbm, groups_ref, local_sem.at[9]),
        pltpu.make_async_copy(
            q_hbm.at[pl.ds(pl.multiple_of(me * piece, piece), piece)],
            q_buf.at[me],
            local_sem.at[10],
        ),
    ]
    for copy in local + late:
        copy.start()
    for s in range(n):

        @pl.when(me != s)
        def _(s=s):
            k_buf[s] = jnp.zeros((held, HEAD_WIDTH), jnp.bfloat16)
            v_buf[s] = jnp.zeros((held, HEAD_WIDTH), jnp.bfloat16)

    barrier = pltpu.get_barrier_semaphore()
    for t in range(n):

        @pl.when((me != t) & (z <= t // 2) & (x <= t % 2))
        def _(t=t):
            pl.semaphore_signal(barrier, inc=1, device_id={"blk": t}, device_id_type=MESH)

    @pl.when(y == 0)
    def _():
        pl.semaphore_signal(barrier, inc=1, device_id={"mp": across}, device_id_type=MESH)

    @pl.when(c == 1)
    def _():
        pl.semaphore_signal(barrier, inc=1, device_id={"mp": sibling}, device_id_type=MESH)

    before = z + x * (z + 1) + y + (1 - c)

    @pl.when(before > 0)
    def _():
        pl.semaphore_wait(barrier, before)

    for t in range(n):

        @pl.when((me != t) & (t // 2 <= z) & (t % 2 <= x))
        def _(t=t):
            pl.semaphore_signal(
                ready_blk.at[me], inc=1, device_id={"blk": t}, device_id_type=MESH
            )

    @pl.when(c == 0)
    def _():
        pl.semaphore_signal(
            ready_mp.at[0], inc=1, device_id={"mp": sibling}, device_id_type=MESH
        )

    @pl.when(y == 1)
    def _():
        pl.semaphore_signal(
            ready_mp.at[1], inc=1, device_id={"mp": across}, device_id_type=MESH
        )

    for copy in local:
        copy.wait()
    meta_buf[me] = meta_buf[me] + (block_ref[0] // per_group) * (n * rows)

    def kv_copy(part, slot, window, target, sem):
        return pltpu.make_async_remote_copy(
            src_ref=bufs[part].at[slot, window],
            dst_ref=bufs[part].at[slot, window],
            send_sem=sem,
            recv_sem=kv_recv.at[slot, part],
            device_id={"blk": target},
            device_id_type=MESH,
        )

    def plane_copy(part, t, whole=False):
        window = pl.ds(0, held) if whole else plane_window(t)
        return kv_copy(part, me, window, 2 * t + x, z_send.at[t, part])

    def cross_copy(part, zz, low):
        slot = 2 * zz + x
        return kv_copy(part, slot, block_window(partner, low), partner, x_send.at[zz, part])

    def pass_copy(part, zz):
        return kv_copy(part, 2 * zz + x, plane_window(3), 6 + x, f_send.at[part])

    def cross(part, zz, act):
        @pl.when(z < lines // 2)
        def _():
            act(cross_copy(part, zz, True))

        @pl.when(z >= lines // 2)
        def _():
            act(cross_copy(part, zz, False))

    def meta_copy(t):
        return pltpu.make_async_remote_copy(
            src_ref=meta_buf.at[me],
            dst_ref=meta_buf.at[me],
            send_sem=meta_send.at[t],
            recv_sem=meta_recv.at[me],
            device_id={"blk": t},
            device_id_type=MESH,
        )

    def q_copy(t):
        return pltpu.make_async_remote_copy(
            src_ref=q_hbm.at[t * piece : (t + 1) * piece],
            dst_ref=q_buf.at[me],
            send_sem=q_send.at[t],
            recv_sem=q_recv.at[me],
            device_id={"blk": t},
            device_id_type=MESH,
        )

    def start(copy):
        copy.start()

    def sent(copy):
        copy.wait_send()

    def to_plane(t, act):
        if t == 2:

            @pl.when(z == 1)
            def _():
                for part in range(2):
                    act(plane_copy(part, t, True))

        ok = z != t
        if t >= 2:
            ok = ok & (z != 1)

        @pl.when(ok)
        def _():
            for part in range(2):
                act(plane_copy(part, t))

    def rest_to(t):
        for xx in range(2):
            meta_copy(2 * t + xx).start()
        for xx in range(2):
            q_copy(2 * t + xx).start()

    for t in range(lines - 1):

        @pl.when(t < z)
        def _(t=t):
            to_plane(t, start)

    @pl.when(x == 0)
    def _():
        pl.semaphore_wait(ready_blk.at[me + 1], 1)

    for part in range(2):
        cross(part, z, start)
    for t in range(n):

        @pl.when(partner == t)
        def _(t=t):
            meta_copy(t).start()
            q_copy(t).start()

    for t in range(lines - 1):

        @pl.when(t < z)
        def _(t=t):
            rest_to(t)

    for t in range(1, lines):

        @pl.when(z < t)
        def _(t=t):
            pl.semaphore_wait(ready_blk.at[2 * t + x], 1)
            to_plane(t, start)

    @pl.when(c == 1)
    def _():
        pl.semaphore_wait(ready_mp.at[0], 1)

    def columns(block):
        return pl.ds(pl.multiple_of(block * width, 128), width)

    w_out = [
        pltpu.make_async_remote_copy(
            src_ref=w_hbm.at[:, columns(block)],
            dst_ref=w_sib.at[i],
            send_sem=wx_send.at[i],
            recv_sem=wx_recv.at[i],
            device_id={"mp": sibling},
            device_id_type=MESH,
        )
        for i, block in enumerate((diagonal, sibling))
    ]
    w_in = [
        pltpu.make_async_copy(w_hbm.at[:, columns(block)], w_own.at[i], w_sem.at[i])
        for i, block in enumerate((across, m))
    ]
    for copy in w_out + w_in:
        copy.start()

    def landed(part, zz, xx, own):
        slot = 2 * zz + xx

        def wait(window):
            kv_copy(part, slot, window, partner, z_send.at[0, part]).wait_recv()

        if own:

            @pl.when(z < 2)
            def _():
                wait(plane_window(0))

            @pl.when((z == 2) & (zz == 1))
            def _():
                wait(pl.ds(0, held))

            @pl.when((z == 3) | ((z == 2) & (zz != 1)))
            def _():
                wait(plane_window(2))

        else:

            @pl.when(z < 2)
            def _():
                kv_copy(
                    part, slot, block_window(me, True), partner, z_send.at[0, part]
                ).wait_recv()

            @pl.when(z >= 2)
            def _():
                kv_copy(
                    part, slot, block_window(me, False), partner, z_send.at[0, part]
                ).wait_recv()

    def relay(zz):
        for part in range(2):
            landed(part, zz, x, True)

            @pl.when((z == 2) & (zz == 1))
            def _(part=part):
                pass_copy(part, zz).start()

            cross(part, zz, start)

    def rest_up(below):
        for t in range(below + 1, lines):

            @pl.when(x == 0)
            def _(t=t):
                pl.semaphore_wait(ready_blk.at[2 * t + 1 - x], 1)

            rest_to(t)

    for plane, sequence in enumerate(((1, 2, -1, 3), (0, 2, -1, 3), (1, 0, -1, 3), (2, 0, 1))):

        @pl.when(z == plane)
        def _(plane=plane, sequence=sequence):
            for zz in sequence:
                if zz < 0:
                    rest_up(plane)
                else:
                    relay(zz)

    for copy in late:
        copy.wait()
    row_ids = lax.broadcasted_iota(jnp.int32, (rows, rows), 0) + me * rows
    start_row = jnp.zeros((rows, rows), jnp.int32)
    group_row = jnp.full((rows, rows), groups_ref[0], jnp.int32)
    end = lengths_ref[0]
    for r in range(1, requests):
        past = row_ids >= end
        start_row = jnp.where(past, end, start_row)
        group_row = jnp.where(past, groups_ref[r], group_row)
        end = end + lengths_ref[r]

    lane = lax.broadcasted_iota(jnp.int32, (1, rows), 1)
    query_row = jnp.zeros((1, rows), jnp.int32)
    meta_rows, meta_groups = [], []
    for s in range(n):

        @pl.when(me != s)
        def _(s=s):
            pltpu.make_async_remote_copy(
                src_ref=meta_buf.at[s],
                dst_ref=meta_buf.at[s],
                send_sem=meta_send.at[s],
                recv_sem=meta_recv.at[s],
                device_id={"blk": partner},
                device_id_type=MESH,
            ).wait_recv()

        meta_rows.append(lax.rem(meta_buf[s], n * rows))
        meta_groups.append(lax.div(meta_buf[s], n * rows))
        shift = lax.rem((s + n - me) * piece, rows)
        turned = pltpu.roll(jnp.broadcast_to(meta_rows[s], (8, rows)), shift, 1)[0:1, :]
        query_row = jnp.where((lane >= s * piece) & (lane < (s + 1) * piece), turned, query_row)
    select = jnp.where(row_ids == query_row, 1.0, 0.0).astype(jnp.bfloat16)
    for s in range(n):

        @pl.when(me != s)
        def _(s=s):
            pltpu.make_async_remote_copy(
                src_ref=q_buf.at[s],
                dst_ref=q_buf.at[s],
                send_sem=q_send.at[s],
                recv_sem=q_recv.at[s],
                device_id={"blk": partner},
                device_id_type=MESH,
            ).wait_recv()

    placed = jnp.dot(
        select, q_buf[...].reshape(rows, -1), preferred_element_type=jnp.float32
    ).astype(jnp.bfloat16)
    for h in range(heads):
        ordered_q[h * rows : (h + 1) * rows, :] = placed[:, h * HEAD_WIDTH : (h + 1) * HEAD_WIDTH]
    scale = LOG2E / math.sqrt(HEAD_WIDTH)

    for zz in range(lines):
        landed(0, zz, 1 - x, False)
    blocks = n + n // 2
    top = None
    for b in range(blocks):
        if b < n:
            keys = jnp.concatenate([k_buf[b, 0:lead], k_buf[b, rest:]], axis=0)
            key_row = meta_rows[b]
            shown = (key_row >= start_row) & (key_row <= row_ids)
        else:
            r = b - n
            keys = k_buf[2 * r : 2 * r + 2, lead:rest].reshape(rows, HEAD_WIDTH)
            key_group = jnp.where(
                lane < rows // 2, meta_groups[2 * r], meta_groups[2 * r + 1]
            )
            shown = key_group == group_row
        scores = (
            lax.dot_general(
                ordered_q[...],
                keys,
                (((1,), (1,)), ((), ())),
                preferred_element_type=jnp.float32,
            )
            * scale
        )
        scores = jnp.where(shown[None], scores.reshape(heads, rows, rows), NEGATIVE)
        score_buf[b] = scores
        top = scores if top is None else jnp.maximum(top, scores)
    top = jnp.max(top, axis=2, keepdims=True)

    for zz in range(lines):
        landed(1, zz, 1 - x, False)
    total = jnp.zeros((heads, rows, rows), jnp.float32)
    for b in range(blocks):
        weights = jnp.exp2(score_buf[b] - top)
        total = total + weights
        weight_buf[:, b * rows : (b + 1) * rows] = weights.astype(jnp.bfloat16).reshape(
            heads * rows, rows
        )
    total = jnp.sum(total, axis=2, keepdims=True).reshape(heads * rows, 1)
    suffix = jnp.concatenate([v_buf[:, 0:lead], v_buf[:, rest:]], axis=1)
    mixed = jnp.dot(
        weight_buf[:, : n * rows],
        suffix.reshape(n * rows, HEAD_WIDTH),
        preferred_element_type=jnp.float32,
    ) + jnp.dot(
        weight_buf[:, n * rows :],
        v_buf[:, lead:rest].reshape(n * rows // 2, HEAD_WIDTH),
        preferred_element_type=jnp.float32,
    )
    mixed = (mixed / total).astype(jnp.bfloat16)
    for h in range(heads):
        att_buf[:, h * HEAD_WIDTH : (h + 1) * HEAD_WIDTH] = mixed[h * rows : (h + 1) * rows]

    att_copy = pltpu.make_async_remote_copy(
        src_ref=att_buf,
        dst_ref=att_sib,
        send_sem=att_send,
        recv_sem=att_recv,
        device_id={"mp": sibling},
        device_id_type=MESH,
    )
    att_copy.start()

    @pl.when(y == 0)
    def _():
        pl.semaphore_wait(ready_mp.at[1], 1)

    chunks = send_buf.shape[0]
    span = width // chunks
    for i in range(2):
        w_in[i].wait()
        w_out[i].wait_recv()
    att_copy.wait_recv()

    def project(i, lanes):
        return jnp.dot(
            att_buf[...], w_own[i, :, lanes], preferred_element_type=jnp.float32
        ) + jnp.dot(att_sib[...], w_sib[i, :, lanes], preferred_element_type=jnp.float32)

    red_copies = []
    for j in range(chunks):
        lanes = slice(j * span, (j + 1) * span)
        send_buf[j] = project(0, lanes).astype(jnp.bfloat16)
        copy = pltpu.make_async_remote_copy(
            src_ref=send_buf.at[j],
            dst_ref=recv_buf.at[j],
            send_sem=red_send.at[j],
            recv_sem=red_recv.at[j],
            device_id={"mp": across},
            device_id_type=MESH,
        )
        copy.start()
        red_copies.append(copy)
    for j in range(chunks):
        part_buf[j] = project(1, slice(j * span, (j + 1) * span))
    for j in range(chunks):
        red_copies[j].wait_recv()
        out_ref[:, j * span : (j + 1) * span] = (
            part_buf[j] + recv_buf[j].astype(jnp.float32)
        ).astype(jnp.bfloat16)

    for t in range(lines):
        to_plane(t, sent)
    for zz in range(lines):
        for part in range(2):
            cross(part, zz, sent)

            if zz == 1:

                @pl.when(z == 2)
                def _(part=part, zz=zz):
                    pass_copy(part, zz).wait_send()

    for t in range(n):

        @pl.when(me != t)
        def _(t=t):
            meta_copy(t).wait_send()
            q_copy(t).wait_send()

    for copy in w_out + red_copies + [att_copy]:
        copy.wait_send()


def shards(
    lengths,
    groups,
    deal,
    prefix_block,
    queries,
    keys,
    values,
    prefix_key_blocks,
    prefix_value_blocks,
    out_weight,
):
    n = lax.axis_size("blk")
    rows = queries.shape[0]
    piece = rows // n
    if n != 8 or rows != 128 or 2 * prefix_key_blocks.shape[0] != rows:
        return plain_shards(
            lengths,
            groups,
            deal,
            prefix_block,
            queries,
            keys,
            values,
            prefix_key_blocks,
            prefix_value_blocks,
            out_weight,
        )
    heads = queries.shape[1] // HEAD_WIDTH
    prefix_rows = prefix_key_blocks.shape[0]
    depth = out_weight.shape[0]
    columns = out_weight.shape[1] // lax.axis_size("mp")
    blocks = n + n // 2
    chunks = 4
    bf16, f32, i32 = jnp.bfloat16, jnp.float32, jnp.int32
    hbm = pl.BlockSpec(memory_space=pltpu.HBM)
    dma = pltpu.SemaphoreType.DMA
    regular = pltpu.SemaphoreType.REGULAR
    operands = (
        lengths,
        groups,
        prefix_block,
        deal.reshape(1, rows),
        queries,
        keys,
        values,
        prefix_key_blocks,
        prefix_value_blocks,
        out_weight,
    )
    return pl.pallas_call(
        functools.partial(fused_kernel, n),
        out_shape=jax.ShapeDtypeStruct((rows, columns), bf16),
        in_specs=[hbm, hbm, pl.BlockSpec(memory_space=pltpu.SMEM)] + [hbm] * (len(operands) - 3),
        out_specs=pl.BlockSpec(memory_space=pltpu.VMEM),
        scratch_shapes=[
            pltpu.SMEM(lengths.shape, i32),
            pltpu.SMEM(groups.shape, i32),
            pltpu.VMEM((n, piece, queries.shape[1]), bf16),
            pltpu.VMEM((heads * rows, HEAD_WIDTH), bf16),
            pltpu.VMEM((n, rows + prefix_rows, HEAD_WIDTH), bf16),
            pltpu.VMEM((n, rows + prefix_rows, HEAD_WIDTH), bf16),
            pltpu.VMEM((2, depth, columns), bf16),
            pltpu.VMEM((2, depth, columns), bf16),
            pltpu.VMEM((n, 1, rows), i32),
            pltpu.VMEM((blocks, heads, rows, rows), f32),
            pltpu.VMEM((heads * rows, blocks * rows), bf16),
            pltpu.VMEM((rows, heads * HEAD_WIDTH), bf16),
            pltpu.VMEM((rows, heads * HEAD_WIDTH), bf16),
            pltpu.VMEM((chunks, rows, columns // chunks), f32),
            pltpu.VMEM((chunks, rows, columns // chunks), bf16),
            pltpu.VMEM((chunks, rows, columns // chunks), bf16),
            dma((11,)),
            dma((2,)),
            regular((n,)),
            regular((2,)),
            dma((n // 2, 2)),
            dma((n // 2, 2)),
            dma((2,)),
            dma((n, 2)),
            dma((n,)),
            dma((n,)),
            dma((n,)),
            dma((n,)),
            dma((2,)),
            dma((2,)),
            dma,
            dma,
            dma((chunks,)),
            dma((chunks,)),
        ],
        compiler_params=pltpu.CompilerParams(
            collective_id=0, has_side_effects=True, vmem_limit_bytes=28 << 20
        ),
    )(
        *[
            v if v is prefix_block else pltpu.with_memory_space_constraint(v, pltpu.HBM)
            for v in operands
        ]
    )


def solution(mesh):
    return jax.shard_map(
        shards,
        mesh=mesh,
        in_specs=(
            P(),
            P(),
            P("blk"),
            P("blk"),
            P("blk", "mp"),
            P("blk", "mp"),
            P("blk", "mp"),
            P("blk", "mp"),
            P("blk", "mp"),
            P("mp", None),
        ),
        out_specs=P("blk", "mp"),
        check_vma=False,
    )
```

```python
import functools
import math

import jax
import jax.numpy as jnp
from jax import lax
from jax.experimental import pallas as pl
from jax.experimental.pallas import tpu as pltpu
from jax.sharding import PartitionSpec as P

HEAD_WIDTH = 128
GROUPS = 4


NEGATIVE = -1e30


def request_index(row_ids, req_ends):
    return jnp.sum((row_ids[:, None] >= req_ends[None, :]).astype(jnp.int32), axis=1)


def lookup(values_table, indices):
    slots = jnp.arange(values_table.shape[0], dtype=jnp.int32)
    return jnp.sum(jnp.where(indices[:, None] == slots[None, :], values_table[None, :], 0), axis=1)


def attend(flash_state, grouped, key_block, value_block, visible):
    run_best, run_total, run_accum = flash_state
    key_count = key_block.shape[0]
    kv_heads = grouped.shape[1]
    head_size = grouped.shape[3]
    score_scale = 1.0 / math.sqrt(head_size)
    keys_three = key_block.reshape(key_count, kv_heads, head_size)
    values_three = value_block.reshape(key_count, kv_heads, head_size)
    scores = (
        jnp.einsum("rgjd,ngd->rgjn", grouped, keys_three, preferred_element_type=jnp.float32)
        * score_scale
    )
    shown = visible[:, None, None, :]
    scores = jnp.where(shown, scores, NEGATIVE)
    new_best = jnp.maximum(run_best, jnp.max(scores, axis=3))
    weights = jnp.where(shown, jnp.exp(scores - new_best[..., None]), 0.0)
    factor = jnp.exp(run_best - new_best)
    run_total = run_total * factor + jnp.sum(weights, axis=3)
    mixed = jnp.einsum(
        "rgjn,ngd->rgjd",
        weights.astype(jnp.bfloat16),
        values_three,
        preferred_element_type=jnp.float32,
    )
    run_accum = run_accum * factor[..., None] + mixed
    return (new_best, run_total, run_accum)


def sweep(flash_state, grouped, key_block, value_block, key_info, visible_of):
    key_count = key_block.shape[0]
    step_width = key_count if key_count <= 1024 else math.gcd(key_count, 512)
    if step_width == key_count:
        return attend(flash_state, grouped, key_block, value_block, visible_of(key_info))

    def one_step(carried, step_index):
        offset = step_index * step_width
        key_part = lax.dynamic_slice_in_dim(key_block, offset, step_width, 0)
        value_part = lax.dynamic_slice_in_dim(value_block, offset, step_width, 0)
        info_part = lax.dynamic_slice_in_dim(key_info, offset, step_width, 0)
        return (attend(carried, grouped, key_part, value_part, visible_of(info_part)), None)

    flash_state, _ = lax.scan(
        one_step, flash_state, jnp.arange(key_count // step_width, dtype=jnp.int32)
    )
    return flash_state


def plain_shards(
    lengths,
    groups,
    deal,
    prefix_block,
    queries,
    keys,
    values,
    prefix_key_blocks,
    prefix_value_blocks,
    out_weight,
):
    count_rows = queries.shape[0]
    kv_heads = keys.shape[1] // HEAD_WIDTH
    query_per_key_head = queries.shape[1] // keys.shape[1]
    devices = lax.axis_size("blk")
    my_index = lax.axis_index("blk")
    piece_rows = count_rows // devices
    per_group = devices // GROUPS
    prefix_rows = prefix_key_blocks.shape[0]
    ranks = jnp.arange(lengths.shape[0], dtype=jnp.int32)
    req_ends = jnp.sum(
        jnp.where(ranks[:, None] >= ranks[None, :], lengths[None, :], 0), axis=1
    ).astype(jnp.int32)
    arrived = lax.all_to_all(
        deal.reshape(devices, piece_rows), "blk", split_axis=0, concat_axis=0, tiled=True
    )
    placed = arrived.reshape(count_rows) - my_index * count_rows

    def prefix_pass(flash_state, grouped, query_group, block_ids):

        def prefix_step(carried, kv_piece):
            key_count = kv_piece[0].shape[0]
            key_group = jnp.broadcast_to(
                (block_ids // per_group)[:, None], (key_count // prefix_rows, prefix_rows)
            ).reshape(key_count)

            def same_group(key_info):
                return key_info[None, :] == query_group[:, None]

            return sweep(carried, grouped, kv_piece[0], kv_piece[1], key_group, same_group)

        return prefix_step(
            flash_state,
            (
                lax.all_gather(prefix_key_blocks, "blk", axis=0, tiled=True),
                lax.all_gather(prefix_value_blocks, "blk", axis=0, tiled=True),
            ),
        )

    def suffix_rule(query_rows, query_req):

        def same_request(key_info):
            key_req = request_index(key_info, req_ends)
            return (
                (key_info[None, :] >= 0)
                & (key_req[None, :] == query_req[:, None])
                & (key_info[None, :] <= query_rows[:, None])
            )

        return same_request

    key_rows, block_ids = (
        lax.all_gather(deal, "blk", axis=0, tiled=True),
        lax.all_gather(prefix_block, "blk", axis=0, tiled=True),
    )
    query_rows = deal
    query_req = request_index(query_rows, req_ends)
    query_group = lookup(groups, query_req)
    grouped = queries.reshape(count_rows, kv_heads, query_per_key_head, HEAD_WIDTH)
    flash_state = prefix_pass(
        (
            jnp.full((count_rows, kv_heads, query_per_key_head), NEGATIVE, jnp.float32),
            jnp.zeros((count_rows, kv_heads, query_per_key_head), jnp.float32),
            jnp.zeros((count_rows, kv_heads, query_per_key_head, HEAD_WIDTH), jnp.float32),
        ),
        grouped,
        query_group,
        block_ids,
    )
    visible_of = suffix_rule(query_rows, query_req)
    kv_piece = (
        lax.all_gather(keys, "blk", axis=0, tiled=True),
        lax.all_gather(values, "blk", axis=0, tiled=True),
    )
    key_info = key_rows
    flash_state = sweep(flash_state, grouped, kv_piece[0], kv_piece[1], key_info, visible_of)
    run_best, run_total, run_accum = flash_state
    attended = (run_accum / run_total[..., None]).astype(jnp.bfloat16).reshape(count_rows, -1)
    returned = lax.all_to_all(
        attended.reshape(devices, piece_rows, -1), "blk", split_axis=0, concat_axis=0, tiled=True
    )
    flat = returned.reshape(count_rows, returned.shape[2])
    turn = placed[None, :] == jnp.arange(count_rows, dtype=jnp.int32)[:, None]
    ordered = jnp.dot(
        turn.astype(flat.dtype), flat, preferred_element_type=jnp.float32
    ).astype(flat.dtype)
    partial_value = jnp.dot(ordered, out_weight, preferred_element_type=jnp.float32)
    return lax.psum_scatter(
        partial_value.astype(jnp.bfloat16), "mp", scatter_dimension=1, tiled=True
    )


LOG2E = 1.4426950408889634


def fused_kernel(
    n,
    lengths_hbm,
    groups_hbm,
    block_ref,
    deal_hbm,
    q_hbm,
    k_hbm,
    v_hbm,
    pk_hbm,
    pv_hbm,
    w_hbm,
    out_ref,
    lengths_ref,
    groups_ref,
    q_buf,
    ordered_q,
    k_buf,
    v_buf,
    w_own,
    w_sib,
    meta_buf,
    score_buf,
    weight_buf,
    att_buf,
    att_sib,
    part_buf,
    send_buf,
    recv_buf,
    local_sem,
    w_sem,
    ready_blk,
    ready_mp,
    go,
    z_send,
    x_send,
    f_send,
    kv_recv,
    meta_send,
    meta_recv,
    q_send,
    q_recv,
    wx_send,
    wx_recv,
    att_send,
    att_recv,
    red_send,
    red_recv,
):
    me = lax.axis_index("blk")
    m = lax.axis_index("mp")
    y = m // 2
    c = m - y * 2
    sibling = y * 2 + (1 - c)
    across = (1 - y) * 2 + c
    diagonal = (1 - y) * 2 + (1 - c)
    z = me // 2
    x = me - z * 2
    partner = z * 2 + 1 - x
    rows = q_hbm.shape[0]
    heads = q_hbm.shape[1] // HEAD_WIDTH
    piece = rows // n
    requests = lengths_hbm.shape[0]
    per_group = n // GROUPS
    width = out_ref.shape[1]
    lines = n // 2
    MESH = pl.DeviceIdType.MESH
    prefix_rows = pk_hbm.shape[0]
    lead = 2 * piece
    rest = lead + prefix_rows
    held = rows + prefix_rows

    def plane_window(t):
        if t == lines - 1:
            return pl.ds(lead, held - lead)
        return pl.ds(0, rest + 2 * t * piece)

    def block_windows(xx, planes):
        cases = []
        for t in planes:
            if t == 0:
                cases.append((z == t, pl.ds(0, rest)))
            elif t == 1:
                cases.append(((z == t) & (xx == 0), pl.ds(0, rest + piece)))
                cases.append(((z == t) & (xx == 1), pl.ds(0, rest + 2 * piece)))
            elif t == 2:
                first = pl.multiple_of(xx * piece, piece)
                cases.append((z == t, pl.ds(first, held - 3 * piece)))
            else:
                cases.append(((z == t) & (xx == 0), pl.ds(lead, held - 3 * piece)))
                cases.append(((z == t) & (xx == 1), pl.ds(lead, held - 2 * piece)))
        return cases

    bufs = (k_buf, v_buf)
    local = [
        pltpu.make_async_copy(k_hbm.at[0:lead], k_buf.at[me, 0:lead], local_sem.at[0]),
        pltpu.make_async_copy(pk_hbm, k_buf.at[me, lead:rest], local_sem.at[1]),
        pltpu.make_async_copy(k_hbm.at[lead:], k_buf.at[me, rest:], local_sem.at[2]),
        pltpu.make_async_copy(v_hbm.at[0:lead], v_buf.at[me, 0:lead], local_sem.at[3]),
        pltpu.make_async_copy(pv_hbm, v_buf.at[me, lead:rest], local_sem.at[4]),
        pltpu.make_async_copy(v_hbm.at[lead:], v_buf.at[me, rest:], local_sem.at[5]),
        pltpu.make_async_copy(deal_hbm, meta_buf.at[me], local_sem.at[6]),
    ]
    late = [
        pltpu.make_async_copy(lengths_hbm, lengths_ref, local_sem.at[8]),
        pltpu.make_async_copy(groups_hbm, groups_ref, local_sem.at[9]),
        pltpu.make_async_copy(
            q_hbm.at[pl.ds(pl.multiple_of(me * piece, piece), piece)],
            q_buf.at[me],
            local_sem.at[10],
        ),
    ]
    for copy in local + late:
        copy.start()
    for s in range(n):

        @pl.when(me != s)
        def _(s=s):
            k_buf[s] = jnp.zeros((held, HEAD_WIDTH), jnp.bfloat16)
            v_buf[s] = jnp.zeros((held, HEAD_WIDTH), jnp.bfloat16)

    barrier = pltpu.get_barrier_semaphore()
    for t in range(n):

        @pl.when((me != t) & (z <= t // 2) & (x <= t % 2))
        def _(t=t):
            pl.semaphore_signal(barrier, inc=1, device_id={"blk": t}, device_id_type=MESH)

    @pl.when(y == 0)
    def _():
        pl.semaphore_signal(barrier, inc=1, device_id={"mp": across}, device_id_type=MESH)

    @pl.when(c == 1)
    def _():
        pl.semaphore_signal(barrier, inc=1, device_id={"mp": sibling}, device_id_type=MESH)

    before = z + x * (z + 1) + y + (1 - c)

    @pl.when(before > 0)
    def _():
        pl.semaphore_wait(barrier, before)

    for t in range(n):

        @pl.when((me != t) & (t // 2 <= z) & (t % 2 <= x))
        def _(t=t):
            pl.semaphore_signal(
                ready_blk.at[me], inc=1, device_id={"blk": t}, device_id_type=MESH
            )

    @pl.when(c == 0)
    def _():
        pl.semaphore_signal(
            ready_mp.at[0], inc=1, device_id={"mp": sibling}, device_id_type=MESH
        )

    @pl.when(y == 1)
    def _():
        pl.semaphore_signal(
            ready_mp.at[1], inc=1, device_id={"mp": across}, device_id_type=MESH
        )

    for copy in local:
        copy.wait()
    meta_buf[me] = meta_buf[me] + (block_ref[0] // per_group) * (n * rows)

    def kv_copy(part, slot, window, target, sem):
        return pltpu.make_async_remote_copy(
            src_ref=bufs[part].at[slot, window],
            dst_ref=bufs[part].at[slot, window],
            send_sem=sem,
            recv_sem=kv_recv.at[slot, part],
            device_id={"blk": target},
            device_id_type=MESH,
        )

    def plane_copy(part, t, whole=False):
        window = pl.ds(0, held) if whole else plane_window(t)
        return kv_copy(part, me, window, 2 * t + x, z_send.at[t, part])

    def pass_copy(part, zz):
        return kv_copy(part, 2 * zz + x, plane_window(3), 6 + x, f_send.at[zz, part])

    def cross(part, zz, act, planes=range(4)):
        slot = 2 * zz + x
        for ok, window in block_windows(1 - x, planes):

            @pl.when(ok)
            def _(window=window):
                act(kv_copy(part, slot, window, partner, x_send.at[zz, part]))

    def meta_copy(t):
        return pltpu.make_async_remote_copy(
            src_ref=meta_buf.at[me],
            dst_ref=meta_buf.at[me],
            send_sem=meta_send.at[t],
            recv_sem=meta_recv.at[me],
            device_id={"blk": t},
            device_id_type=MESH,
        )

    def q_copy(t):
        return pltpu.make_async_remote_copy(
            src_ref=q_hbm.at[t * piece : (t + 1) * piece],
            dst_ref=q_buf.at[me],
            send_sem=q_send.at[t],
            recv_sem=q_recv.at[me],
            device_id={"blk": t},
            device_id_type=MESH,
        )

    def start(copy):
        copy.start()

    def sent(copy):
        copy.wait_send()

    def to_plane(t, act):
        if t == 2:

            @pl.when(z <= 1)
            def _():
                for part in range(2):
                    act(plane_copy(part, t, True))

        ok = z != t
        if t >= 2:
            ok = ok & (z > 1)

        @pl.when(ok)
        def _():
            for part in range(2):
                act(plane_copy(part, t))

    def rest_to(t):
        for xx in range(2):
            meta_copy(2 * t + xx).start()
        for xx in range(2):
            q_copy(2 * t + xx).start()

    for t in range(lines - 1):

        @pl.when(t < z)
        def _(t=t):
            to_plane(t, start)

    @pl.when(x == 0)
    def _():
        pl.semaphore_wait(ready_blk.at[me + 1], 1)

    for part in range(2):
        cross(part, z, start)
    for t in range(n):

        @pl.when(partner == t)
        def _(t=t):
            meta_copy(t).start()
            q_copy(t).start()

    for t in range(lines - 1):

        @pl.when((t < z) & (c == 0))
        def _(t=t):
            rest_to(t)

    for t in range(1, lines):

        @pl.when(z < t)
        def _(t=t):
            pl.semaphore_wait(ready_blk.at[2 * t + x], 1)
            to_plane(t, start)

    @pl.when(c == 1)
    def _():
        pl.semaphore_wait(ready_mp.at[0], 1)

    def columns(block):
        return pl.ds(pl.multiple_of(block * width, 128), width)

    w_out = [
        pltpu.make_async_remote_copy(
            src_ref=w_hbm.at[:, columns(block)],
            dst_ref=w_sib.at[i],
            send_sem=wx_send.at[i],
            recv_sem=wx_recv.at[i],
            device_id={"mp": sibling},
            device_id_type=MESH,
        )
        for i, block in enumerate((diagonal, sibling))
    ]
    w_in = [
        pltpu.make_async_copy(w_hbm.at[:, columns(block)], w_own.at[i], w_sem.at[i])
        for i, block in enumerate((across, m))
    ]
    for copy in w_out + w_in:
        copy.start()

    def landed(part, zz, xx, own, planes=()):
        slot = 2 * zz + xx

        def wait(window):
            kv_copy(part, slot, window, partner, z_send.at[0, part]).wait_recv()

        if own:
            for t in planes:

                @pl.when(z == t)
                def _(t=t):
                    wait(pl.ds(0, held) if t == 2 and zz <= 1 else plane_window(t))

        else:
            for ok, window in block_windows(x, range(lines)):

                @pl.when(ok)
                def _(window=window):
                    wait(window)

    def relay(zz, plane):
        for part in range(2):
            landed(part, zz, x, True, (plane,))
            if plane == 2 and zz <= 1:
                pass_copy(part, zz).start()
            cross(part, zz, start, (plane,))

    def rest_up(below):
        for t in range(below + 1, lines):

            @pl.when(x == 0)
            def _(t=t):
                pl.semaphore_wait(ready_blk.at[2 * t + 1 - x], 1)

            rest_to(t)

    for plane, sequence in enumerate(((1, -2, 2, -1, 3, -3), (0, -2, 2, -1, 3, -3), (1, -2, 0, -1, 3, -3), (-2, -3, 2, 1, 0))):

        @pl.when(z == plane)
        def _(plane=plane, sequence=sequence):
            for zz in sequence:
                if zz == -1:

                    @pl.when(c == 0)
                    def _():
                        rest_up(plane)

                elif zz == -2:

                    @pl.when(c == 0)
                    def _():
                        pl.semaphore_signal(
                            go, inc=1, device_id={"mp": sibling}, device_id_type=MESH
                        )

                elif zz == -3:

                    @pl.when(c == 1)
                    def _():
                        pl.semaphore_wait(go, 1)
                        for t in range(plane):
                            rest_to(t)
                        rest_up(plane)

                else:
                    relay(zz, plane)

    for copy in late:
        copy.wait()
    row_ids = lax.broadcasted_iota(jnp.int32, (rows, rows), 0) + me * rows
    start_row = jnp.zeros((rows, rows), jnp.int32)
    group_row = jnp.full((rows, rows), groups_ref[0], jnp.int32)
    end = lengths_ref[0]
    for r in range(1, requests):
        past = row_ids >= end
        start_row = jnp.where(past, end, start_row)
        group_row = jnp.where(past, groups_ref[r], group_row)
        end = end + lengths_ref[r]

    lane = lax.broadcasted_iota(jnp.int32, (1, rows), 1)
    query_row = jnp.zeros((1, rows), jnp.int32)
    meta_rows, meta_groups = [], []
    for s in range(n):

        @pl.when(me != s)
        def _(s=s):
            pltpu.make_async_remote_copy(
                src_ref=meta_buf.at[s],
                dst_ref=meta_buf.at[s],
                send_sem=meta_send.at[s],
                recv_sem=meta_recv.at[s],
                device_id={"blk": partner},
                device_id_type=MESH,
            ).wait_recv()

        meta_rows.append(lax.rem(meta_buf[s], n * rows))
        meta_groups.append(lax.div(meta_buf[s], n * rows))
        shift = lax.rem((s + n - me) * piece, rows)
        turned = pltpu.roll(jnp.broadcast_to(meta_rows[s], (8, rows)), shift, 1)[0:1, :]
        query_row = jnp.where((lane >= s * piece) & (lane < (s + 1) * piece), turned, query_row)
    select = jnp.where(row_ids == query_row, 1.0, 0.0).astype(jnp.bfloat16)
    for s in range(n):

        @pl.when(me != s)
        def _(s=s):
            pltpu.make_async_remote_copy(
                src_ref=q_buf.at[s],
                dst_ref=q_buf.at[s],
                send_sem=q_send.at[s],
                recv_sem=q_recv.at[s],
                device_id={"blk": partner},
                device_id_type=MESH,
            ).wait_recv()

    placed = jnp.dot(
        select, q_buf[...].reshape(rows, -1), preferred_element_type=jnp.float32
    ).astype(jnp.bfloat16)
    half = rows // 2
    for i in range(2):
        for h in range(heads):
            ordered_q[i, h * half : (h + 1) * half, :] = placed[
                i * half : (i + 1) * half, h * HEAD_WIDTH : (h + 1) * HEAD_WIDTH
            ]
    scale = LOG2E / math.sqrt(HEAD_WIDTH)

    for zz in range(lines):
        landed(0, zz, 1 - x, False)
    blocks = n + n // 2

    def attention(i):
        part = slice(i * half, (i + 1) * half)
        top = None
        for b in range(blocks):
            if b < n:
                keys = jnp.concatenate([k_buf[b, 0:lead], k_buf[b, rest:]], axis=0)
                shown = (meta_rows[b] >= start_row[part]) & (meta_rows[b] <= row_ids[part])
            else:
                r = b - n
                keys = k_buf[2 * r : 2 * r + 2, lead:rest].reshape(rows, HEAD_WIDTH)
                key_group = jnp.where(
                    lane < rows // 2, meta_groups[2 * r], meta_groups[2 * r + 1]
                )
                shown = key_group == group_row[part]
            scores = (
                lax.dot_general(
                    ordered_q[i],
                    keys,
                    (((1,), (1,)), ((), ())),
                    preferred_element_type=jnp.float32,
                )
                * scale
            )
            scores = jnp.where(shown[None], scores.reshape(heads, half, rows), NEGATIVE)
            score_buf[b] = scores
            top = scores if top is None else jnp.maximum(top, scores)
        top = jnp.max(top, axis=2, keepdims=True)
        total = jnp.zeros((heads, half, rows), jnp.float32)
        for b in range(blocks):
            weights = jnp.exp2(score_buf[b] - top)
            total = total + weights
            weight_buf[:, b * rows : (b + 1) * rows] = weights.astype(jnp.bfloat16).reshape(
                heads * half, rows
            )
        total = jnp.sum(total, axis=2, keepdims=True).reshape(heads * half, 1)
        if i == 0:
            for zz in range(lines):
                landed(1, zz, 1 - x, False)
        suffix = jnp.concatenate([v_buf[:, 0:lead], v_buf[:, rest:]], axis=1)
        mixed = jnp.dot(
            weight_buf[:, : n * rows],
            suffix.reshape(n * rows, HEAD_WIDTH),
            preferred_element_type=jnp.float32,
        ) + jnp.dot(
            weight_buf[:, n * rows :],
            v_buf[:, lead:rest].reshape(n * rows // 2, HEAD_WIDTH),
            preferred_element_type=jnp.float32,
        )
        mixed = (mixed / total).astype(jnp.bfloat16)
        for h in range(heads):
            att_buf[part, h * HEAD_WIDTH : (h + 1) * HEAD_WIDTH] = mixed[
                h * half : (h + 1) * half
            ]

    att_copies = [
        pltpu.make_async_remote_copy(
            src_ref=att_buf.at[i * half : (i + 1) * half],
            dst_ref=att_sib.at[i * half : (i + 1) * half],
            send_sem=att_send.at[i],
            recv_sem=att_recv.at[i],
            device_id={"mp": sibling},
            device_id_type=MESH,
        )
        for i in range(2)
    ]
    for i in range(2):
        attention(i)
        att_copies[i].start()

    @pl.when(y == 0)
    def _():
        pl.semaphore_wait(ready_mp.at[1], 1)

    chunks = send_buf.shape[1]
    span = width // chunks
    for i in range(2):
        w_in[i].wait()
        w_out[i].wait_recv()

    def project(i, part, lanes):
        return jnp.dot(
            att_buf[part], w_own[i, :, lanes], preferred_element_type=jnp.float32
        ) + jnp.dot(att_sib[part], w_sib[i, :, lanes], preferred_element_type=jnp.float32)

    red_copies = []
    for i in range(2):
        att_copies[i].wait_recv()
        for j in range(chunks):
            send_buf[i, j] = project(
                0, slice(i * half, (i + 1) * half), slice(j * span, (j + 1) * span)
            ).astype(jnp.bfloat16)
            copy = pltpu.make_async_remote_copy(
                src_ref=send_buf.at[i, j],
                dst_ref=recv_buf.at[i, j],
                send_sem=red_send.at[i, j],
                recv_sem=red_recv.at[i, j],
                device_id={"mp": across},
                device_id_type=MESH,
            )
            copy.start()
            red_copies.append(copy)
    for j in range(chunks):
        part_buf[j] = project(1, slice(0, rows), slice(j * span, (j + 1) * span))
    for i in range(2):
        part = slice(i * half, (i + 1) * half)
        for j in range(chunks):
            red_copies[i * chunks + j].wait_recv()
            out_ref[part, j * span : (j + 1) * span] = (
                part_buf[j, part] + recv_buf[i, j].astype(jnp.float32)
            ).astype(jnp.bfloat16)

    for t in range(lines):
        to_plane(t, sent)
    for zz in range(lines):
        for part in range(2):
            cross(part, zz, sent)

            if zz <= 1:

                @pl.when(z == 2)
                def _(part=part, zz=zz):
                    pass_copy(part, zz).wait_send()

    for t in range(n):

        @pl.when(me != t)
        def _(t=t):
            meta_copy(t).wait_send()
            q_copy(t).wait_send()

    for copy in w_out + red_copies + att_copies:
        copy.wait_send()


def shards(
    lengths,
    groups,
    deal,
    prefix_block,
    queries,
    keys,
    values,
    prefix_key_blocks,
    prefix_value_blocks,
    out_weight,
):
    n = lax.axis_size("blk")
    rows = queries.shape[0]
    piece = rows // n
    if n != 8 or rows != 128 or 2 * prefix_key_blocks.shape[0] != rows:
        return plain_shards(
            lengths,
            groups,
            deal,
            prefix_block,
            queries,
            keys,
            values,
            prefix_key_blocks,
            prefix_value_blocks,
            out_weight,
        )
    heads = queries.shape[1] // HEAD_WIDTH
    prefix_rows = prefix_key_blocks.shape[0]
    depth = out_weight.shape[0]
    columns = out_weight.shape[1] // lax.axis_size("mp")
    blocks = n + n // 2
    chunks = 2
    bf16, f32, i32 = jnp.bfloat16, jnp.float32, jnp.int32
    hbm = pl.BlockSpec(memory_space=pltpu.HBM)
    dma = pltpu.SemaphoreType.DMA
    regular = pltpu.SemaphoreType.REGULAR
    operands = (
        lengths,
        groups,
        prefix_block,
        deal.reshape(1, rows),
        queries,
        keys,
        values,
        prefix_key_blocks,
        prefix_value_blocks,
        out_weight,
    )
    return pl.pallas_call(
        functools.partial(fused_kernel, n),
        out_shape=jax.ShapeDtypeStruct((rows, columns), bf16),
        in_specs=[hbm, hbm, pl.BlockSpec(memory_space=pltpu.SMEM)] + [hbm] * (len(operands) - 3),
        out_specs=pl.BlockSpec(memory_space=pltpu.VMEM),
        scratch_shapes=[
            pltpu.SMEM(lengths.shape, i32),
            pltpu.SMEM(groups.shape, i32),
            pltpu.VMEM((n, piece, queries.shape[1]), bf16),
            pltpu.VMEM((2, heads * rows // 2, HEAD_WIDTH), bf16),
            pltpu.VMEM((n, rows + prefix_rows, HEAD_WIDTH), bf16),
            pltpu.VMEM((n, rows + prefix_rows, HEAD_WIDTH), bf16),
            pltpu.VMEM((2, depth, columns), bf16),
            pltpu.VMEM((2, depth, columns), bf16),
            pltpu.VMEM((n, 1, rows), i32),
            pltpu.VMEM((blocks, heads, rows // 2, rows), f32),
            pltpu.VMEM((heads * rows // 2, blocks * rows), bf16),
            pltpu.VMEM((rows, heads * HEAD_WIDTH), bf16),
            pltpu.VMEM((rows, heads * HEAD_WIDTH), bf16),
            pltpu.VMEM((chunks, rows, columns // chunks), f32),
            pltpu.VMEM((2, chunks, rows // 2, columns // chunks), bf16),
            pltpu.VMEM((2, chunks, rows // 2, columns // chunks), bf16),
            dma((11,)),
            dma((2,)),
            regular((n,)),
            regular((2,)),
            regular,
            dma((n // 2, 2)),
            dma((n // 2, 2)),
            dma((2, 2)),
            dma((n, 2)),
            dma((n,)),
            dma((n,)),
            dma((n,)),
            dma((n,)),
            dma((2,)),
            dma((2,)),
            dma((2,)),
            dma((2,)),
            dma((2, chunks)),
            dma((2, chunks)),
        ],
        compiler_params=pltpu.CompilerParams(
            collective_id=0, has_side_effects=True, vmem_limit_bytes=28 << 20
        ),
    )(
        *[
            v if v is prefix_block else pltpu.with_memory_space_constraint(v, pltpu.HBM)
            for v in operands
        ]
    )


def solution(mesh):
    return jax.shard_map(
        shards,
        mesh=mesh,
        in_specs=(
            P(),
            P(),
            P("blk"),
            P("blk"),
            P("blk", "mp"),
            P("blk", "mp"),
            P("blk", "mp"),
            P("blk", "mp"),
            P("blk", "mp"),
            P("mp", None),
        ),
        out_specs=P("blk", "mp"),
        check_vma=False,
    )
```

```python
import functools
import math

import jax
import jax.numpy as jnp
from jax import lax
from jax.experimental import pallas as pl
from jax.experimental.pallas import tpu as pltpu
from jax.sharding import PartitionSpec as P

HEAD_WIDTH = 128
GROUPS = 4


NEGATIVE = -1e30


def request_index(row_ids, req_ends):
    return jnp.sum((row_ids[:, None] >= req_ends[None, :]).astype(jnp.int32), axis=1)


def lookup(values_table, indices):
    slots = jnp.arange(values_table.shape[0], dtype=jnp.int32)
    return jnp.sum(jnp.where(indices[:, None] == slots[None, :], values_table[None, :], 0), axis=1)


def attend(flash_state, grouped, key_block, value_block, visible):
    run_best, run_total, run_accum = flash_state
    key_count = key_block.shape[0]
    kv_heads = grouped.shape[1]
    head_size = grouped.shape[3]
    score_scale = 1.0 / math.sqrt(head_size)
    keys_three = key_block.reshape(key_count, kv_heads, head_size)
    values_three = value_block.reshape(key_count, kv_heads, head_size)
    scores = (
        jnp.einsum("rgjd,ngd->rgjn", grouped, keys_three, preferred_element_type=jnp.float32)
        * score_scale
    )
    shown = visible[:, None, None, :]
    scores = jnp.where(shown, scores, NEGATIVE)
    new_best = jnp.maximum(run_best, jnp.max(scores, axis=3))
    weights = jnp.where(shown, jnp.exp(scores - new_best[..., None]), 0.0)
    factor = jnp.exp(run_best - new_best)
    run_total = run_total * factor + jnp.sum(weights, axis=3)
    mixed = jnp.einsum(
        "rgjn,ngd->rgjd",
        weights.astype(jnp.bfloat16),
        values_three,
        preferred_element_type=jnp.float32,
    )
    run_accum = run_accum * factor[..., None] + mixed
    return (new_best, run_total, run_accum)


def sweep(flash_state, grouped, key_block, value_block, key_info, visible_of):
    key_count = key_block.shape[0]
    step_width = key_count if key_count <= 1024 else math.gcd(key_count, 512)
    if step_width == key_count:
        return attend(flash_state, grouped, key_block, value_block, visible_of(key_info))

    def one_step(carried, step_index):
        offset = step_index * step_width
        key_part = lax.dynamic_slice_in_dim(key_block, offset, step_width, 0)
        value_part = lax.dynamic_slice_in_dim(value_block, offset, step_width, 0)
        info_part = lax.dynamic_slice_in_dim(key_info, offset, step_width, 0)
        return (attend(carried, grouped, key_part, value_part, visible_of(info_part)), None)

    flash_state, _ = lax.scan(
        one_step, flash_state, jnp.arange(key_count // step_width, dtype=jnp.int32)
    )
    return flash_state


def plain_shards(
    lengths,
    groups,
    deal,
    prefix_block,
    queries,
    keys,
    values,
    prefix_key_blocks,
    prefix_value_blocks,
    out_weight,
):
    count_rows = queries.shape[0]
    kv_heads = keys.shape[1] // HEAD_WIDTH
    query_per_key_head = queries.shape[1] // keys.shape[1]
    devices = lax.axis_size("blk")
    my_index = lax.axis_index("blk")
    piece_rows = count_rows // devices
    per_group = devices // GROUPS
    prefix_rows = prefix_key_blocks.shape[0]
    ranks = jnp.arange(lengths.shape[0], dtype=jnp.int32)
    req_ends = jnp.sum(
        jnp.where(ranks[:, None] >= ranks[None, :], lengths[None, :], 0), axis=1
    ).astype(jnp.int32)
    arrived = lax.all_to_all(
        deal.reshape(devices, piece_rows), "blk", split_axis=0, concat_axis=0, tiled=True
    )
    placed = arrived.reshape(count_rows) - my_index * count_rows

    def prefix_pass(flash_state, grouped, query_group, block_ids):

        def prefix_step(carried, kv_piece):
            key_count = kv_piece[0].shape[0]
            key_group = jnp.broadcast_to(
                (block_ids // per_group)[:, None], (key_count // prefix_rows, prefix_rows)
            ).reshape(key_count)

            def same_group(key_info):
                return key_info[None, :] == query_group[:, None]

            return sweep(carried, grouped, kv_piece[0], kv_piece[1], key_group, same_group)

        return prefix_step(
            flash_state,
            (
                lax.all_gather(prefix_key_blocks, "blk", axis=0, tiled=True),
                lax.all_gather(prefix_value_blocks, "blk", axis=0, tiled=True),
            ),
        )

    def suffix_rule(query_rows, query_req):

        def same_request(key_info):
            key_req = request_index(key_info, req_ends)
            return (
                (key_info[None, :] >= 0)
                & (key_req[None, :] == query_req[:, None])
                & (key_info[None, :] <= query_rows[:, None])
            )

        return same_request

    key_rows, block_ids = (
        lax.all_gather(deal, "blk", axis=0, tiled=True),
        lax.all_gather(prefix_block, "blk", axis=0, tiled=True),
    )
    query_rows = deal
    query_req = request_index(query_rows, req_ends)
    query_group = lookup(groups, query_req)
    grouped = queries.reshape(count_rows, kv_heads, query_per_key_head, HEAD_WIDTH)
    flash_state = prefix_pass(
        (
            jnp.full((count_rows, kv_heads, query_per_key_head), NEGATIVE, jnp.float32),
            jnp.zeros((count_rows, kv_heads, query_per_key_head), jnp.float32),
            jnp.zeros((count_rows, kv_heads, query_per_key_head, HEAD_WIDTH), jnp.float32),
        ),
        grouped,
        query_group,
        block_ids,
    )
    visible_of = suffix_rule(query_rows, query_req)
    kv_piece = (
        lax.all_gather(keys, "blk", axis=0, tiled=True),
        lax.all_gather(values, "blk", axis=0, tiled=True),
    )
    key_info = key_rows
    flash_state = sweep(flash_state, grouped, kv_piece[0], kv_piece[1], key_info, visible_of)
    run_best, run_total, run_accum = flash_state
    attended = (run_accum / run_total[..., None]).astype(jnp.bfloat16).reshape(count_rows, -1)
    returned = lax.all_to_all(
        attended.reshape(devices, piece_rows, -1), "blk", split_axis=0, concat_axis=0, tiled=True
    )
    flat = returned.reshape(count_rows, returned.shape[2])
    turn = placed[None, :] == jnp.arange(count_rows, dtype=jnp.int32)[:, None]
    ordered = jnp.dot(
        turn.astype(flat.dtype), flat, preferred_element_type=jnp.float32
    ).astype(flat.dtype)
    partial_value = jnp.dot(ordered, out_weight, preferred_element_type=jnp.float32)
    return lax.psum_scatter(
        partial_value.astype(jnp.bfloat16), "mp", scatter_dimension=1, tiled=True
    )


LOG2E = 1.4426950408889634


def fused_kernel(
    n,
    lengths_hbm,
    groups_hbm,
    block_ref,
    deal_hbm,
    q_hbm,
    k_hbm,
    v_hbm,
    pk_hbm,
    pv_hbm,
    w_hbm,
    out_ref,
    lengths_ref,
    groups_ref,
    q_buf,
    ordered_q,
    k_buf,
    v_buf,
    w_own,
    w_sib,
    meta_buf,
    score_buf,
    weight_buf,
    att_buf,
    att_sib,
    part_buf,
    send_buf,
    recv_buf,
    local_sem,
    w_sem,
    ready_blk,
    ready_mp,
    go,
    z_send,
    x_send,
    f_send,
    s_send,
    kv_recv,
    meta_send,
    meta_recv,
    q_send,
    q_recv,
    wx_send,
    wx_recv,
    att_send,
    att_recv,
    red_send,
    red_recv,
):
    me = lax.axis_index("blk")
    m = lax.axis_index("mp")
    y = m // 2
    c = m - y * 2
    sibling = y * 2 + (1 - c)
    across = (1 - y) * 2 + c
    diagonal = (1 - y) * 2 + (1 - c)
    z = me // 2
    x = me - z * 2
    partner = z * 2 + 1 - x
    rows = q_hbm.shape[0]
    heads = q_hbm.shape[1] // HEAD_WIDTH
    piece = rows // n
    requests = lengths_hbm.shape[0]
    per_group = n // GROUPS
    width = out_ref.shape[1]
    lines = n // 2
    MESH = pl.DeviceIdType.MESH
    prefix_rows = pk_hbm.shape[0]
    lead = 2 * piece
    rest = lead + prefix_rows
    held = rows + prefix_rows

    def plane_window(t):
        if t == lines - 1:
            return pl.ds(lead, held - lead)
        return pl.ds(0, rest + 2 * t * piece)

    def block_windows(xx, planes):
        cases = []
        for t in planes:
            if t == 0:
                cases.append((z == t, pl.ds(0, rest)))
            elif t == 1:
                cases.append(((z == t) & (xx == 0), pl.ds(0, rest + piece)))
                cases.append(((z == t) & (xx == 1), pl.ds(0, rest + 2 * piece)))
            elif t == 2:
                first = pl.multiple_of(xx * piece, piece)
                cases.append((z == t, pl.ds(first, held - 3 * piece)))
            else:
                cases.append(((z == t) & (xx == 0), pl.ds(lead, held - 3 * piece)))
                cases.append(((z == t) & (xx == 1), pl.ds(lead, held - 2 * piece)))
        return cases

    bufs = (k_buf, v_buf)
    local = [
        pltpu.make_async_copy(k_hbm.at[0:lead], k_buf.at[me, 0:lead], local_sem.at[0]),
        pltpu.make_async_copy(pk_hbm, k_buf.at[me, lead:rest], local_sem.at[1]),
        pltpu.make_async_copy(k_hbm.at[lead:], k_buf.at[me, rest:], local_sem.at[2]),
        pltpu.make_async_copy(v_hbm.at[0:lead], v_buf.at[me, 0:lead], local_sem.at[3]),
        pltpu.make_async_copy(pv_hbm, v_buf.at[me, lead:rest], local_sem.at[4]),
        pltpu.make_async_copy(v_hbm.at[lead:], v_buf.at[me, rest:], local_sem.at[5]),
        pltpu.make_async_copy(deal_hbm, meta_buf.at[me], local_sem.at[6]),
    ]
    late = [
        pltpu.make_async_copy(lengths_hbm, lengths_ref, local_sem.at[8]),
        pltpu.make_async_copy(groups_hbm, groups_ref, local_sem.at[9]),
        pltpu.make_async_copy(
            q_hbm.at[pl.ds(pl.multiple_of(me * piece, piece), piece)],
            q_buf.at[me],
            local_sem.at[10],
        ),
    ]
    for copy in local + late:
        copy.start()
    for s in range(n):

        @pl.when(me != s)
        def _(s=s):
            k_buf[s] = jnp.zeros((held, HEAD_WIDTH), jnp.bfloat16)
            v_buf[s] = jnp.zeros((held, HEAD_WIDTH), jnp.bfloat16)

    barrier = pltpu.get_barrier_semaphore()
    for t in range(n):

        @pl.when((me != t) & (z <= t // 2) & (x <= t % 2))
        def _(t=t):
            pl.semaphore_signal(barrier, inc=1, device_id={"blk": t}, device_id_type=MESH)

    @pl.when(y == 0)
    def _():
        pl.semaphore_signal(barrier, inc=1, device_id={"mp": across}, device_id_type=MESH)

    @pl.when(c == 1)
    def _():
        pl.semaphore_signal(barrier, inc=1, device_id={"mp": sibling}, device_id_type=MESH)

    before = z + x * (z + 1) + y + (1 - c)

    @pl.when(before > 0)
    def _():
        pl.semaphore_wait(barrier, before)

    for t in range(n):

        @pl.when((me != t) & (t // 2 <= z) & (t % 2 <= x))
        def _(t=t):
            pl.semaphore_signal(
                ready_blk.at[me], inc=1, device_id={"blk": t}, device_id_type=MESH
            )

    @pl.when(c == 0)
    def _():
        pl.semaphore_signal(
            ready_mp.at[0], inc=1, device_id={"mp": sibling}, device_id_type=MESH
        )

    @pl.when(y == 1)
    def _():
        pl.semaphore_signal(
            ready_mp.at[1], inc=1, device_id={"mp": across}, device_id_type=MESH
        )

    for copy in local:
        copy.wait()
    meta_buf[me] = meta_buf[me] + (block_ref[0] // per_group) * (n * rows)

    def kv_copy(part, slot, window, target, sem):
        return pltpu.make_async_remote_copy(
            src_ref=bufs[part].at[slot, window],
            dst_ref=bufs[part].at[slot, window],
            send_sem=sem,
            recv_sem=kv_recv.at[slot, part],
            device_id={"blk": target},
            device_id_type=MESH,
        )

    def plane_copy(part, t, whole=False):
        window = pl.ds(0, held) if whole else plane_window(t)
        return kv_copy(part, me, window, 2 * t + x, z_send.at[t, part])

    def skip_copy(part, zz):
        window = pl.ds(lead, held - 3 * piece)
        return kv_copy(part, 2 * zz + 1, window, n - 2, s_send.at[zz, part])

    def pass_copy(part, zz):
        return kv_copy(part, 2 * zz + x, plane_window(3), 6 + x, f_send.at[zz, part])

    def cross(part, zz, act, planes=range(4)):
        slot = 2 * zz + x
        for ok, window in block_windows(1 - x, planes):
            if isinstance(zz, int) and zz in (0,):
                ok = ok & ((z < 3) | (x == 0) | (c == 1))

            @pl.when(ok)
            def _(window=window):
                act(kv_copy(part, slot, window, partner, x_send.at[zz, part]))

    def meta_copy(t):
        return pltpu.make_async_remote_copy(
            src_ref=meta_buf.at[me],
            dst_ref=meta_buf.at[me],
            send_sem=meta_send.at[t],
            recv_sem=meta_recv.at[me],
            device_id={"blk": t},
            device_id_type=MESH,
        )

    def q_copy(t):
        return pltpu.make_async_remote_copy(
            src_ref=q_hbm.at[t * piece : (t + 1) * piece],
            dst_ref=q_buf.at[me],
            send_sem=q_send.at[t],
            recv_sem=q_recv.at[me],
            device_id={"blk": t},
            device_id_type=MESH,
        )

    def start(copy):
        copy.start()

    def sent(copy):
        copy.wait_send()

    def to_plane(t, act):
        if t == 2:

            @pl.when(z <= 1)
            def _():
                for part in range(2):
                    act(plane_copy(part, t, True))

        ok = z != t
        if t >= 2:
            ok = ok & (z > 1)

        @pl.when(ok)
        def _():
            for part in range(2):
                act(plane_copy(part, t))

    def rest_to(t):
        for xx in range(2):
            meta_copy(2 * t + xx).start()
        for xx in range(2):
            q_copy(2 * t + xx).start()

    for t in range(lines - 1):

        @pl.when(t < z)
        def _(t=t):
            to_plane(t, start)

    @pl.when(x == 0)
    def _():
        pl.semaphore_wait(ready_blk.at[me + 1], 1)

    for part in range(2):
        cross(part, z, start)
    for t in range(n):

        @pl.when(partner == t)
        def _(t=t):
            meta_copy(t).start()
            q_copy(t).start()

    for t in range(lines - 1):

        @pl.when((t < z) & (c == 0))
        def _(t=t):
            rest_to(t)

    for t in range(1, lines):

        @pl.when(z < t)
        def _(t=t):
            pl.semaphore_wait(ready_blk.at[2 * t + x], 1)
            to_plane(t, start)

    @pl.when(c == 1)
    def _():
        pl.semaphore_wait(ready_mp.at[0], 1)

    def columns(block):
        return pl.ds(pl.multiple_of(block * width, 128), width)

    w_out = [
        pltpu.make_async_remote_copy(
            src_ref=w_hbm.at[:, columns(block)],
            dst_ref=w_sib.at[i],
            send_sem=wx_send.at[i],
            recv_sem=wx_recv.at[i],
            device_id={"mp": sibling},
            device_id_type=MESH,
        )
        for i, block in enumerate((diagonal, sibling))
    ]
    w_in = [
        pltpu.make_async_copy(w_hbm.at[:, columns(block)], w_own.at[i], w_sem.at[i])
        for i, block in enumerate((across, m))
    ]
    for copy in w_out + w_in:
        copy.start()

    def landed(part, zz, xx, own, planes=()):
        slot = 2 * zz + xx

        def wait(window):
            kv_copy(part, slot, window, partner, z_send.at[0, part]).wait_recv()

        if own:
            for t in planes:

                @pl.when(z == t)
                def _(t=t):
                    wait(pl.ds(0, held) if t == 2 and zz <= 1 else plane_window(t))

        else:
            for ok, window in block_windows(x, range(lines)):

                @pl.when(ok)
                def _(window=window):
                    wait(window)

    def relay(zz, plane):
        for part in range(2):
            landed(part, zz, x, True, (plane,))
            if plane == 2 and zz <= 1:
                if zz in (0,):

                    @pl.when((x == 1) & (c == 0))
                    def _(part=part, zz=zz):
                        skip_copy(part, zz).start()

                pass_copy(part, zz).start()
            cross(part, zz, start, (plane,))

    def rest_up(below):
        for t in range(below + 1, lines):

            @pl.when(x == 0)
            def _(t=t):
                pl.semaphore_wait(ready_blk.at[2 * t + 1 - x], 1)

            rest_to(t)

    for plane, sequence in enumerate(((1, -2, 2, -1, 3, -3), (0, -2, 2, -1, 3, -3), (1, -2, 0, -1, -3, 3), (-2, -3, 2, 1, 0))):

        @pl.when(z == plane)
        def _(plane=plane, sequence=sequence):
            for zz in sequence:
                if zz == -1:

                    @pl.when(c == 0)
                    def _():
                        rest_up(plane)

                elif zz == -2:

                    @pl.when(c == 0)
                    def _():
                        pl.semaphore_signal(
                            go, inc=1, device_id={"mp": sibling}, device_id_type=MESH
                        )

                elif zz == -3:

                    @pl.when(c == 1)
                    def _():
                        pl.semaphore_wait(go, 1)
                        for t in range(plane):
                            rest_to(t)
                        rest_up(plane)

                else:
                    relay(zz, plane)

    for copy in late:
        copy.wait()
    row_ids = lax.broadcasted_iota(jnp.int32, (rows, rows), 0) + me * rows
    start_row = jnp.zeros((rows, rows), jnp.int32)
    group_row = jnp.full((rows, rows), groups_ref[0], jnp.int32)
    end = lengths_ref[0]
    for r in range(1, requests):
        past = row_ids >= end
        start_row = jnp.where(past, end, start_row)
        group_row = jnp.where(past, groups_ref[r], group_row)
        end = end + lengths_ref[r]

    lane = lax.broadcasted_iota(jnp.int32, (1, rows), 1)
    query_row = jnp.zeros((1, rows), jnp.int32)
    meta_rows, meta_groups = [], []
    for s in range(n):

        @pl.when(me != s)
        def _(s=s):
            pltpu.make_async_remote_copy(
                src_ref=meta_buf.at[s],
                dst_ref=meta_buf.at[s],
                send_sem=meta_send.at[s],
                recv_sem=meta_recv.at[s],
                device_id={"blk": partner},
                device_id_type=MESH,
            ).wait_recv()

        meta_rows.append(lax.rem(meta_buf[s], n * rows))
        meta_groups.append(lax.div(meta_buf[s], n * rows))
        shift = lax.rem((s + n - me) * piece, rows)
        turned = pltpu.roll(jnp.broadcast_to(meta_rows[s], (8, rows)), shift, 1)[0:1, :]
        query_row = jnp.where((lane >= s * piece) & (lane < (s + 1) * piece), turned, query_row)
    select = jnp.where(row_ids == query_row, 1.0, 0.0).astype(jnp.bfloat16)
    for s in range(n):

        @pl.when(me != s)
        def _(s=s):
            pltpu.make_async_remote_copy(
                src_ref=q_buf.at[s],
                dst_ref=q_buf.at[s],
                send_sem=q_send.at[s],
                recv_sem=q_recv.at[s],
                device_id={"blk": partner},
                device_id_type=MESH,
            ).wait_recv()

    placed = jnp.dot(
        select, q_buf[...].reshape(rows, -1), preferred_element_type=jnp.float32
    ).astype(jnp.bfloat16)
    half = rows // 2
    for i in range(2):
        for h in range(heads):
            ordered_q[i, h * half : (h + 1) * half, :] = placed[
                i * half : (i + 1) * half, h * HEAD_WIDTH : (h + 1) * HEAD_WIDTH
            ]
    scale = LOG2E / math.sqrt(HEAD_WIDTH)

    for zz in range(lines):
        landed(0, zz, 1 - x, False)
    blocks = n + n // 2

    def attention(i):
        part = slice(i * half, (i + 1) * half)
        top = None
        for b in range(blocks):
            if b < n:
                keys = jnp.concatenate([k_buf[b, 0:lead], k_buf[b, rest:]], axis=0)
                shown = (meta_rows[b] >= start_row[part]) & (meta_rows[b] <= row_ids[part])
            else:
                r = b - n
                keys = k_buf[2 * r : 2 * r + 2, lead:rest].reshape(rows, HEAD_WIDTH)
                key_group = jnp.where(
                    lane < rows // 2, meta_groups[2 * r], meta_groups[2 * r + 1]
                )
                shown = key_group == group_row[part]
            scores = (
                lax.dot_general(
                    ordered_q[i],
                    keys,
                    (((1,), (1,)), ((), ())),
                    preferred_element_type=jnp.float32,
                )
                * scale
            )
            scores = jnp.where(shown[None], scores.reshape(heads, half, rows), NEGATIVE)
            score_buf[b] = scores
            top = scores if top is None else jnp.maximum(top, scores)
        top = jnp.max(top, axis=2, keepdims=True)
        total = jnp.zeros((heads, half, rows), jnp.float32)
        for b in range(blocks):
            weights = jnp.exp2(score_buf[b] - top)
            total = total + weights
            weight_buf[:, b * rows : (b + 1) * rows] = weights.astype(jnp.bfloat16).reshape(
                heads * half, rows
            )
        total = jnp.sum(total, axis=2, keepdims=True).reshape(heads * half, 1)
        if i == 0:
            for zz in range(lines):
                landed(1, zz, 1 - x, False)
        suffix = jnp.concatenate([v_buf[:, 0:lead], v_buf[:, rest:]], axis=1)
        mixed = jnp.dot(
            weight_buf[:, : n * rows],
            suffix.reshape(n * rows, HEAD_WIDTH),
            preferred_element_type=jnp.float32,
        ) + jnp.dot(
            weight_buf[:, n * rows :],
            v_buf[:, lead:rest].reshape(n * rows // 2, HEAD_WIDTH),
            preferred_element_type=jnp.float32,
        )
        mixed = (mixed / total).astype(jnp.bfloat16)
        for h in range(heads):
            att_buf[part, h * HEAD_WIDTH : (h + 1) * HEAD_WIDTH] = mixed[
                h * half : (h + 1) * half
            ]

    att_copies = [
        pltpu.make_async_remote_copy(
            src_ref=att_buf.at[i * half : (i + 1) * half],
            dst_ref=att_sib.at[i * half : (i + 1) * half],
            send_sem=att_send.at[i],
            recv_sem=att_recv.at[i],
            device_id={"mp": sibling},
            device_id_type=MESH,
        )
        for i in range(2)
    ]
    for i in range(2):
        attention(i)
        att_copies[i].start()

    @pl.when(y == 0)
    def _():
        pl.semaphore_wait(ready_mp.at[1], 1)

    chunks = send_buf.shape[1]
    span = width // chunks
    for i in range(2):
        w_in[i].wait()
        w_out[i].wait_recv()

    def project(i, part, lanes):
        return jnp.dot(
            att_buf[part], w_own[i, :, lanes], preferred_element_type=jnp.float32
        ) + jnp.dot(att_sib[part], w_sib[i, :, lanes], preferred_element_type=jnp.float32)

    def keep():
        for j in range(chunks):
            part_buf[j] = project(1, slice(0, rows), slice(j * span, (j + 1) * span))

    red_copies = []
    for i in range(2):
        att_copies[i].wait_recv()
        if i == 1:

            @pl.when(c == 1)
            def _():
                keep()

        for j in range(chunks):
            send_buf[i, j] = project(
                0, slice(i * half, (i + 1) * half), slice(j * span, (j + 1) * span)
            ).astype(jnp.bfloat16)
            copy = pltpu.make_async_remote_copy(
                src_ref=send_buf.at[i, j],
                dst_ref=recv_buf.at[i, j],
                send_sem=red_send.at[i, j],
                recv_sem=red_recv.at[i, j],
                device_id={"mp": across},
                device_id_type=MESH,
            )
            copy.start()
            red_copies.append(copy)

    @pl.when(c == 0)
    def _():
        keep()

    for i in range(2):
        part = slice(i * half, (i + 1) * half)
        for j in range(chunks):
            red_copies[i * chunks + j].wait_recv()
            out_ref[part, j * span : (j + 1) * span] = (
                part_buf[j, part] + recv_buf[i, j].astype(jnp.float32)
            ).astype(jnp.bfloat16)

    for t in range(lines):
        to_plane(t, sent)
    for zz in range(lines):
        for part in range(2):
            cross(part, zz, sent)

            if zz <= 1:

                @pl.when(z == 2)
                def _(part=part, zz=zz):
                    pass_copy(part, zz).wait_send()

            if zz in (0,):

                @pl.when((z == 2) & (x == 1) & (c == 0))
                def _(part=part, zz=zz):
                    skip_copy(part, zz).wait_send()

    for t in range(n):

        @pl.when(me != t)
        def _(t=t):
            meta_copy(t).wait_send()
            q_copy(t).wait_send()

    for copy in w_out + red_copies + att_copies:
        copy.wait_send()


def shards(
    lengths,
    groups,
    deal,
    prefix_block,
    queries,
    keys,
    values,
    prefix_key_blocks,
    prefix_value_blocks,
    out_weight,
):
    n = lax.axis_size("blk")
    rows = queries.shape[0]
    piece = rows // n
    if n != 8 or rows != 128 or 2 * prefix_key_blocks.shape[0] != rows:
        return plain_shards(
            lengths,
            groups,
            deal,
            prefix_block,
            queries,
            keys,
            values,
            prefix_key_blocks,
            prefix_value_blocks,
            out_weight,
        )
    heads = queries.shape[1] // HEAD_WIDTH
    prefix_rows = prefix_key_blocks.shape[0]
    depth = out_weight.shape[0]
    columns = out_weight.shape[1] // lax.axis_size("mp")
    blocks = n + n // 2
    chunks = 2
    bf16, f32, i32 = jnp.bfloat16, jnp.float32, jnp.int32
    hbm = pl.BlockSpec(memory_space=pltpu.HBM)
    dma = pltpu.SemaphoreType.DMA
    regular = pltpu.SemaphoreType.REGULAR
    operands = (
        lengths,
        groups,
        prefix_block,
        deal.reshape(1, rows),
        queries,
        keys,
        values,
        prefix_key_blocks,
        prefix_value_blocks,
        out_weight,
    )
    return pl.pallas_call(
        functools.partial(fused_kernel, n),
        out_shape=jax.ShapeDtypeStruct((rows, columns), bf16),
        in_specs=[hbm, hbm, pl.BlockSpec(memory_space=pltpu.SMEM)] + [hbm] * (len(operands) - 3),
        out_specs=pl.BlockSpec(memory_space=pltpu.VMEM),
        scratch_shapes=[
            pltpu.SMEM(lengths.shape, i32),
            pltpu.SMEM(groups.shape, i32),
            pltpu.VMEM((n, piece, queries.shape[1]), bf16),
            pltpu.VMEM((2, heads * rows // 2, HEAD_WIDTH), bf16),
            pltpu.VMEM((n, rows + prefix_rows, HEAD_WIDTH), bf16),
            pltpu.VMEM((n, rows + prefix_rows, HEAD_WIDTH), bf16),
            pltpu.VMEM((2, depth, columns), bf16),
            pltpu.VMEM((2, depth, columns), bf16),
            pltpu.VMEM((n, 1, rows), i32),
            pltpu.VMEM((blocks, heads, rows // 2, rows), f32),
            pltpu.VMEM((heads * rows // 2, blocks * rows), bf16),
            pltpu.VMEM((rows, heads * HEAD_WIDTH), bf16),
            pltpu.VMEM((rows, heads * HEAD_WIDTH), bf16),
            pltpu.VMEM((chunks, rows, columns // chunks), f32),
            pltpu.VMEM((2, chunks, rows // 2, columns // chunks), bf16),
            pltpu.VMEM((2, chunks, rows // 2, columns // chunks), bf16),
            dma((11,)),
            dma((2,)),
            regular((n,)),
            regular((2,)),
            regular,
            dma((n // 2, 2)),
            dma((n // 2, 2)),
            dma((2, 2)),
            dma((2, 2)),
            dma((n, 2)),
            dma((n,)),
            dma((n,)),
            dma((n,)),
            dma((n,)),
            dma((2,)),
            dma((2,)),
            dma((2,)),
            dma((2,)),
            dma((2, chunks)),
            dma((2, chunks)),
        ],
        compiler_params=pltpu.CompilerParams(
            collective_id=0, has_side_effects=True, vmem_limit_bytes=28 << 20
        ),
    )(
        *[
            v if v is prefix_block else pltpu.with_memory_space_constraint(v, pltpu.HBM)
            for v in operands
        ]
    )


def solution(mesh):
    return jax.shard_map(
        shards,
        mesh=mesh,
        in_specs=(
            P(),
            P(),
            P("blk"),
            P("blk"),
            P("blk", "mp"),
            P("blk", "mp"),
            P("blk", "mp"),
            P("blk", "mp"),
            P("blk", "mp"),
            P("mp", None),
        ),
        out_specs=P("blk", "mp"),
        check_vma=False,
    )
```
